32 devices in a mesh: row: 4 (over y, core), col: 8 (over z, x).
Axes of the slice: x: 2, y: 2, z: 4, core: 2. Of those that a mesh axis runs over, the one named last changes fastest.
Arguments:
- stored: float32 [40, 4, 128, 20, 8, 128], P(None, 'row', None, None, 'col'), may hold values from -1 to 13, as said below
- rhs: float32 [20, 8, 128, 128], P(None, 'col'), may hold values from -60 to 60
Outputs:
- solution: float32 [20, 8, 128, 128], P(None, 'col')
- residual: float32 [20, 8, 128, 128], P(None, 'col')
The draws below stay inside these ranges and needn't reach their ends.
Inputs may be any that keep to these rules, and one draw needn't show every extreme that they name: `stored`: the operator A built from it as in the reference program is symmetric positive definite.
All inputs are finite; a program needn't handle non-finite values.
Results may differ from the reference program's by a relative error of at most 0.0003.
Values sent between devices are 32-bit elements; how exact they have to be, the bound alone decides.
No kernel may reach another device: no remote copies, remote signals or barrier semaphores. Data moves between devices by JAX's collectives and lax.ppermute only.
A program may use at most 192 MiB of HBM per device.

```python
import math
import jax
import jax.numpy as jnp
from jax import lax

NORD = 20480
BS = 128
K = 128
ITERS = 2
NB = 160
LR = 40
LC = 20


def draw_stored(key, part):
    noise_key, diag_key = jax.random.split(key, 2)
    entries = jax.random.truncated_normal(noise_key, -6.0, 6.0, (NORD, NORD), jnp.float32)
    entries = entries / math.sqrt(NORD)
    diagonal = jax.random.uniform(diag_key, (NORD,), jnp.float32, 3.0, 5.0)
    flattened = entries.reshape(-1).at[jnp.arange(NORD, dtype=jnp.int32) * (NORD + 1)].set(diagonal)
    matrix = flattened.reshape(NORD, NORD)
    return matrix.reshape(LR, NB // LR, BS, LC, NB // LC, BS)


def draw_rhs(key, part):
    base_key, row_key, col_key = jax.random.split(key, 3)
    row_scale = jnp.exp(jax.random.uniform(row_key, (NORD,), jnp.float32, math.log(0.3), math.log(3.0)))
    col_scale = jnp.exp(jax.random.uniform(col_key, (K,), jnp.float32, math.log(0.3), math.log(3.0)))
    values = jax.random.truncated_normal(base_key, -4.0, 4.0, (NORD, K), jnp.float32)
    values = values * row_scale[:, None] * col_scale[None, :]
    return values.reshape(LC, NB // LC, BS, K)


def setup_inputs(seed: int = 0) -> dict:
    splits = jax.random.split(jax.random.key(seed), 3)
    stored = draw_stored(jax.random.fold_in(splits[2], 71), 0)
    rhs = draw_rhs(jax.random.fold_in(splits[2], 71), 0)
    return dict(stored=stored, rhs=rhs)


HIGHEST = lax.Precision.HIGHEST

def gram_local(left_side, right_side):
    return jnp.dot(left_side.T.astype(jnp.float32), right_side.astype(jnp.float32), precision=HIGHEST, preferred_element_type=jnp.float32)

def mix_right(vectors, matrix):
    return jnp.dot(vectors.astype(jnp.float32), matrix.astype(jnp.float32), precision=HIGHEST, preferred_element_type=jnp.float32)

def solve_spd(matrix, target):
    factor = jnp.linalg.cholesky(matrix)
    return jax.scipy.linalg.cho_solve((factor, True), target)

def reference(stored, rhs):
    block_count = NORD // BS
    blocks = stored.reshape(block_count, BS, block_count, BS)
    indices = jnp.arange(block_count, dtype=jnp.int32)
    weight = jnp.where(indices[:, None] > indices[None, :], 1.0, jnp.where(indices[:, None] == indices[None, :], 0.5, 0.0)).astype(jnp.float32)
    lower_part = (blocks * weight[:, None, :, None]).reshape(NORD, NORD)
    operator = lower_part + lower_part.T
    right_side = rhs.reshape(NORD, K)
    solution = jnp.zeros_like(right_side)
    residual = right_side
    direction = right_side
    gram_now = gram_local(residual, residual)
    for iteration in range(ITERS):
        applied = jnp.dot(operator.astype(jnp.float32), direction.astype(jnp.float32), precision=HIGHEST, preferred_element_type=jnp.float32)
        curvature = gram_local(direction, applied)
        step_size = solve_spd(curvature, gram_now)
        solution = solution + mix_right(direction, step_size)
        residual = residual - mix_right(applied, step_size)
        if iteration + 1 < ITERS:
            gram_next = gram_local(residual, residual)
            mix_factor = solve_spd(gram_now, gram_next)
            direction = residual + mix_right(direction, mix_factor)
            gram_now = gram_next
    return (solution.reshape(rhs.shape), residual.reshape(rhs.shape))
```

```python
import functools

import jax
import jax.numpy as jnp
from jax import lax
from jax.experimental import pallas as pl
from jax.experimental.pallas import tpu as pltpu
from jax.sharding import PartitionSpec as P

ITERS = 2
HIGHEST = lax.Precision.HIGHEST
F32 = jnp.float32
BF16 = jnp.bfloat16
WHOLE = pl.BlockSpec(memory_space=pltpu.VMEM)
SCALARS = pl.BlockSpec(memory_space=pltpu.SMEM)


def params(limit=60 * 1024 * 1024):
    return pltpu.CompilerParams(vmem_limit_bytes=limit)


def exchange(value, axis, mask):
    pairs = [(source, source ^ mask) for source in range(lax.axis_size(axis))]
    return lax.ppermute(value, axis, pairs)


def swap(value):
    rows_n = lax.axis_size("row")
    cols_n = lax.axis_size("col")
    pairs = []
    for r in range(rows_n):
        for c in range(cols_n):
            h, q = divmod(c, rows_n)
            pairs.append((r * cols_n + c, q * cols_n + h * rows_n + r))
    return lax.ppermute(value, ("row", "col"), pairs)


def gather_col(piece):
    cols_n = lax.axis_size("col")
    got = {0: piece}
    for m in sorted(range(2, cols_n, 2), reverse=True):
        got[m] = exchange(piece, "col", m)
    got[1] = exchange(piece, "col", 1)
    for m in range(2, cols_n, 2):
        got[m + 1] = exchange(got[m], "col", 1)
    return [got[m] for m in range(cols_n)]


def scatter_col(pieces):
    cols_n = len(pieces)
    order = sorted(range(0, cols_n, 2), reverse=True)
    arrived = {m: exchange(pieces[m + 1], "col", 1) for m in order}
    total = None
    for m in order:
        part = pieces[m] + arrived[m]
        if m:
            part = exchange(part, "col", m)
        total = part if total is None else total + part
    return total


def gather_row(piece):
    rows_n = lax.axis_size("row")
    got = {0: piece}
    mask = rows_n // 2
    while mask:
        for m in list(got):
            got[m + mask] = exchange(got[m], "row", mask)
        mask //= 2
    return [got[m] for m in range(rows_n)]


def scatter_row(pieces):
    rows_n = len(pieces)
    held = dict(enumerate(pieces))
    mask = 1
    while mask < rows_n:
        sent = {m: exchange(held[m], "row", mask) for m in held if m & mask}
        held = {m: held[m] + sent[m | mask] for m in held if not m & mask}
        mask *= 2
    return held[0]


def sum_over(value, axes):
    for axis in axes:
        mask = 1
        while mask < lax.axis_size(axis):
            value = value + exchange(value, axis, mask)
            mask *= 2
    return value


def gram(left_side, right_side):
    return jnp.einsum(
        "nk,nl->kl", left_side, right_side, precision=HIGHEST, preferred_element_type=F32
    )


def mix(vectors, matrix):
    return jnp.dot(vectors, matrix, precision=HIGHEST, preferred_element_type=F32)


def factor_of(matrix):
    return jnp.linalg.cholesky(matrix)


def solve_with(factor, target):
    return jax.scipy.linalg.cho_solve((factor, True), target)


def split(value):
    high = value.astype(BF16)
    return high, (value - high.astype(F32)).astype(BF16)


def dot(left_side, right_side):
    return jnp.dot(left_side, right_side, preferred_element_type=F32)


class Shape:
    def __init__(self, stored, rhs, rows_n, cols_n):
        self.rows_n, self.cols_n = rows_n, cols_n
        self.groups = cols_n // rows_n
        self.bs = stored.shape[2]
        self.col_blocks = stored.shape[3]
        self.k = rhs.shape[-1]
        self.per = 2 if self.col_blocks % 2 == 0 else 1
        self.tile = self.per * self.bs
        self.n = self.col_blocks // self.per
        self.odd = self.n % 2
        self.pairs = (self.n + self.odd) // 2
        self.width = (self.n + 1 - self.odd) * self.tile
        self.colset = self.col_blocks * self.bs
        self.unit = self.colset // rows_n

    def strips(self, pair):
        out = [(self.n - 1 - pair, 0, self.n - pair)]
        if pair - self.odd >= 0:
            out.append((pair - self.odd, self.n - pair, pair - self.odd + 1))
        return out


def pack_kernel(sh, diag_ref, long_ref, short_ref, hi_ref, lo_ref):
    h, pair = pl.program_id(0), pl.program_id(1)
    blocks, bs = sh.col_blocks, sh.bs

    def tile(source, tile_col, out_tile, on_diag):
        for a in range(sh.per):
            for b in range(sh.per):
                rows = slice(a * bs, (a + 1) * bs)
                cols = pl.ds(pl.multiple_of(out_tile * sh.tile + b * bs, bs), bs)
                if on_diag and a < b:
                    hi_ref[rows, cols] = jnp.zeros((bs, bs), BF16)
                    lo_ref[rows, cols] = jnp.zeros((bs, bs), BF16)
                    continue
                block = source[a, pl.ds(tile_col * sh.per + b, bs, stride=blocks), :]
                if on_diag and a == b:
                    block = block * diag_ref[h]
                high, low = split(block)
                hi_ref[rows, cols] = high
                lo_ref[rows, cols] = low

    def strip(source, tile_row, first):
        def step(j, carry):
            tile(source, j, first + j, False)
            return carry

        lax.fori_loop(0, tile_row, step, 0)
        tile(source, tile_row, first + tile_row, True)

    strip(long_ref, sh.n - 1 - pair, 0)
    if sh.odd:
        @pl.when(pair >= 1)
        def _():
            strip(short_ref, pair - 1, sh.n - pair)
    else:
        strip(short_ref, pair, sh.n - pair)


def pack(sh, stored, diag):
    view = stored.reshape(sh.col_blocks, sh.groups, sh.bs * sh.col_blocks, sh.bs)
    block = (sh.per, None, sh.bs * sh.col_blocks, sh.bs)
    out_block = (None, None, sh.tile, sh.width)
    shape = jax.ShapeDtypeStruct((sh.groups, sh.pairs, sh.tile, sh.width), BF16)
    size = sh.groups * sh.pairs * sh.tile * sh.width
    return pl.pallas_call(
        functools.partial(pack_kernel, sh),
        grid=(sh.groups, sh.pairs),
        in_specs=[
            SCALARS,
            pl.BlockSpec(block, lambda h, q: (sh.n - 1 - q, h, 0, 0)),
            pl.BlockSpec(block, lambda h, q: (jnp.maximum(q - sh.odd, 0), h, 0, 0)),
        ],
        out_specs=[pl.BlockSpec(out_block, lambda h, q: (h, q, 0, 0))] * 2,
        out_shape=[shape, shape],
        compiler_params=params(),
        cost_estimate=pl.CostEstimate(
            flops=4 * size, bytes_accessed=4 * stored.size + 4 * size, transcendentals=0
        ),
        name="pack_lower",
    )(diag, view, view)


def combined(first, second, weights):
    k = first.shape[-1]
    high, low = split(jnp.concatenate([first, second], axis=1))
    both = dot(high, weights[...])
    return both[:, :k] + both[:, k:] + dot(low, weights[:, :k])


def rows_kernel(sh, mixing, *refs):
    refs = list(refs)
    index_ref = refs.pop(0)
    hi_ref, lo_ref = refs.pop(0), refs.pop(0)
    start_ref = refs.pop(0)
    image_refs = [refs.pop(0) for _ in range(sh.rows_n)] if mixing else []
    weight_ref = refs.pop(0) if mixing else None
    out_refs = [refs.pop(0) for _ in range(sh.cols_n)]
    vector_ref = refs.pop(0) if mixing else None
    halves, total = refs.pop(0), refs.pop(0)
    h, pair = pl.program_id(0), pl.program_id(1)
    k, t = sh.k, sh.tile

    @pl.when((h == 0) & (pair == 0))
    def _():
        if mixing:
            for m, image in enumerate(image_refs):
                where = pl.ds(pl.multiple_of((index_ref[0] ^ m) * sh.unit, 8), sh.unit)
                vector_ref[where, :] = combined(start_ref[where, :], image[...], weight_ref)
            source = vector_ref
        else:
            source = start_ref
        high, low = split(source[...])
        halves[:, :k] = high
        halves[:, k:] = low

    for pair_now in range(sh.pairs):
        @pl.when(pair == pair_now)
        def _():
            for tile_row, first, count in sh.strips(pair_now):
                cols = slice(first * t, (first + count) * t)
                both = dot(hi_ref[:, cols], halves[: count * t, :])
                rest = dot(lo_ref[:, cols], halves[: count * t, :k])
                where = pl.ds(pl.multiple_of(h * sh.colset + tile_row * t, 8), t)
                total[where, :] = both[:, :k] + both[:, k:] + rest

    @pl.when((h == sh.groups - 1) & (pair == sh.pairs - 1))
    def _():
        for m, out in enumerate(out_refs):
            where = pl.ds(pl.multiple_of((index_ref[1] ^ m) * sh.unit, 8), sh.unit)
            out[...] = total[where, :]


def packed_specs(sh):
    block = (None, None, sh.tile, sh.width)
    return [pl.BlockSpec(block, lambda h, q: (h, q, 0, 0))] * 2


def product_cost(sh):
    size = sh.groups * sh.pairs * sh.tile * sh.width
    return pl.CostEstimate(flops=6 * size * sh.k, bytes_accessed=4 * size, transcendentals=0)


def apply_rows(sh, index, packed, start, images=None, weights=None):
    mixing = images is not None
    extra = [*images, weights] if mixing else []
    piece = jax.ShapeDtypeStruct((sh.unit, sh.k), F32)
    outs = [piece] * sh.cols_n
    if mixing:
        outs.append(jax.ShapeDtypeStruct((sh.colset, sh.k), F32))
    got = pl.pallas_call(
        functools.partial(rows_kernel, sh, mixing),
        grid=(sh.groups, sh.pairs),
        in_specs=[SCALARS, *packed_specs(sh), WHOLE, *[WHOLE] * len(extra)],
        out_specs=[WHOLE] * len(outs),
        out_shape=outs,
        scratch_shapes=[
            pltpu.VMEM((sh.colset, 2 * sh.k), BF16),
            pltpu.VMEM((sh.groups * sh.colset, sh.k), F32),
        ],
        compiler_params=params(),
        cost_estimate=product_cost(sh),
        name="lower_times",
    )(index, *packed, start, *extra)
    return got[: sh.cols_n], (got[sh.cols_n] if mixing else start)


def cols_kernel(sh, mixing, *refs):
    refs = list(refs)
    index_ref = refs.pop(0)
    hi_ref, lo_ref = refs.pop(0), refs.pop(0)
    column_ref = refs.pop(0)
    start_refs = [refs.pop(0) for _ in range(sh.cols_n)]
    image_refs = [refs.pop(0) for _ in range(sh.cols_n)] if mixing else []
    weight_ref = refs.pop(0) if mixing else None
    out_refs = [refs.pop(0) for _ in range(sh.rows_n)]
    curve_ref = refs.pop(0)
    vector, total, turned = refs
    h, pair = pl.program_id(0), pl.program_id(1)
    k, t = sh.k, sh.tile

    @pl.when((h == 0) & (pair == 0))
    def _():
        for m in range(sh.cols_n):
            where = pl.ds(pl.multiple_of((index_ref[1] ^ m) * sh.unit, 8), sh.unit)
            if mixing:
                vector[where, :] = combined(start_refs[m][...], image_refs[m][...], weight_ref)
            else:
                vector[where, :] = start_refs[m][...]
        total[...] = jnp.zeros_like(total)

    for pair_now in range(sh.pairs):
        @pl.when(pair == pair_now)
        def _():
            for tile_row, first, count in sh.strips(pair_now):
                where = pl.ds(pl.multiple_of(h * sh.colset + tile_row * t, 8), t)
                high, low = split(vector[where, :].T)
                stacked = jnp.concatenate([high, low], axis=0)
                for j in range(count):
                    cols = slice((first + j) * t, (first + j + 1) * t)
                    both = dot(stacked, hi_ref[:, cols])
                    rest = dot(high, lo_ref[:, cols])
                    total[:, j * t : (j + 1) * t] += both[:k] + both[k:] + rest

    @pl.when((h == sh.groups - 1) & (pair == sh.pairs - 1))
    def _():
        turned[...] = total[...].T
        for m, out in enumerate(out_refs):
            where = pl.ds(pl.multiple_of((index_ref[0] ^ m) * sh.unit, 8), sh.unit)
            out[...] = turned[where, :]
        curve_ref[...] = jnp.dot(
            total[...], column_ref[...], precision=HIGHEST, preferred_element_type=F32
        )


def apply_cols(sh, index, packed, column, starts, images=None, weights=None):
    mixing = images is not None
    extra = [*images, weights] if mixing else []
    piece = jax.ShapeDtypeStruct((sh.unit, sh.k), F32)
    outs = [piece] * sh.rows_n + [jax.ShapeDtypeStruct((sh.k, sh.k), F32)]
    got = pl.pallas_call(
        functools.partial(cols_kernel, sh, mixing),
        grid=(sh.groups, sh.pairs),
        in_specs=[SCALARS, *packed_specs(sh), WHOLE, *[WHOLE] * (len(starts) + len(extra))],
        out_specs=[WHOLE] * len(outs),
        out_shape=outs,
        scratch_shapes=[
            pltpu.VMEM((sh.groups * sh.colset, sh.k), F32),
            pltpu.VMEM((sh.k, sh.colset), F32),
            pltpu.VMEM((sh.colset, sh.k), F32),
        ],
        compiler_params=params(),
        cost_estimate=product_cost(sh),
        name="upper_times",
    )(index, *packed, column, *starts, *extra)
    return got[: sh.rows_n], got[sh.rows_n]


def weights_kernel(first_ref, second_ref, out_ref):
    k = first_ref.shape[-1]
    for base, ref in ((0, first_ref), (k, second_ref)):
        high, low = split(ref[...])
        out_ref[base : base + k, :k] = high
        out_ref[base : base + k, k:] = low


def split_weights(first, second):
    k = first.shape[-1]
    return pl.pallas_call(
        weights_kernel,
        in_specs=[WHOLE, WHOLE],
        out_specs=WHOLE,
        out_shape=jax.ShapeDtypeStruct((2 * k, 2 * k), BF16),
        name="split_weights",
    )(first, second)


def order_kernel(sh, index_ref, *refs):
    out_ref = refs[-1]
    for m, piece in enumerate(refs[:-1]):
        where = pl.ds(pl.multiple_of((index_ref[0] ^ m) * sh.unit, 8), sh.unit)
        out_ref[where, :] = piece[...]


def in_order(sh, index, pieces):
    return pl.pallas_call(
        functools.partial(order_kernel, sh),
        in_specs=[SCALARS, *[WHOLE] * len(pieces)],
        out_specs=WHOLE,
        out_shape=jax.ShapeDtypeStruct((sh.colset, sh.k), F32),
        compiler_params=params(),
        name="in_order",
    )(index, *pieces)


def per_device(stored, rhs):
    row_index = lax.axis_index("row")
    col_index = lax.axis_index("col")
    rows_n = lax.axis_size("row")
    cols_n = lax.axis_size("col")
    sh = Shape(stored, rhs, rows_n, cols_n)
    everywhere = ("row", "col")
    index = jnp.stack([row_index, col_index]).astype(jnp.int32)
    offsets = jnp.arange(sh.groups, dtype=jnp.int32) * rows_n + row_index - col_index
    diag = jnp.where(offsets > 0, 1.0, jnp.where(offsets == 0, 0.5, 0.0)).astype(F32)

    start = rhs.reshape(sh.colset, sh.k)
    start_piece = lax.dynamic_slice_in_dim(start, row_index * sh.unit, sh.unit, 0)
    start_rows = gather_col(swap(start_piece))
    packed = pack(sh, stored, diag)
    gram_now = sum_over(gram(start, start), ("col",))
    gram_factor = factor_of(gram_now)

    row_parts, _ = apply_rows(sh, index, packed, start)
    row_piece = scatter_col(row_parts)
    col_parts, curve = apply_cols(sh, index, packed, start, start_rows)
    curve = sum_over(curve, everywhere)
    step_size = solve_with(factor_of(curve + curve.T), gram_now)
    col_piece = scatter_row(col_parts)
    image_piece = col_piece + swap(row_piece)
    image_far = row_piece + swap(col_piece)
    image_rows = gather_col(image_far)
    image_cols = gather_row(image_piece)
    residual_piece = start_piece - mix(image_piece, step_size)
    gram_next = sum_over(gram(residual_piece, residual_piece), everywhere)
    mix_factor = solve_with(gram_factor, gram_next)

    weights = split_weights(jnp.eye(sh.k, dtype=F32) + mix_factor, -step_size)
    row_parts, direction = apply_rows(sh, index, packed, start, image_cols, weights)
    row_piece = scatter_col(row_parts)
    col_parts, curve = apply_cols(
        sh, index, packed, direction, start_rows, image_rows, weights
    )
    curve = sum_over(curve, everywhere)
    last_step = solve_with(factor_of(curve + curve.T), gram_next)
    answer = mix(start, step_size) + mix(direction, last_step)
    image_piece = scatter_row(col_parts) + swap(row_piece)
    residual_piece = residual_piece - mix(image_piece, last_step)
    residual = in_order(sh, index, gather_row(residual_piece))
    return answer.reshape(rhs.shape), residual.reshape(rhs.shape)


def solution(mesh):
    placed = (P(None, "row", None, None, "col", None), P(None, "col", None, None))
    return jax.shard_map(
        per_device,
        mesh=mesh,
        in_specs=placed,
        out_specs=(P(None, "col", None, None), P(None, "col", None, None)),
        check_vma=False,
    )
```

```python
import functools

import jax
import jax.numpy as jnp
from jax import lax
from jax.experimental import pallas as pl
from jax.experimental.pallas import tpu as pltpu
from jax.sharding import PartitionSpec as P


HIGHEST = lax.Precision.HIGHEST
F32 = jnp.float32
BF16 = jnp.bfloat16
WHOLE = pl.BlockSpec(memory_space=pltpu.VMEM)
SCALARS = pl.BlockSpec(memory_space=pltpu.SMEM)


def params(limit=60 * 1024 * 1024):
    return pltpu.CompilerParams(vmem_limit_bytes=limit)


def exchange(value, axis, mask):
    pairs = [(source, source ^ mask) for source in range(lax.axis_size(axis))]
    return lax.ppermute(value, axis, pairs)


def swap(value):
    rows_n = lax.axis_size("row")
    cols_n = lax.axis_size("col")
    pairs = []
    for r in range(rows_n):
        for c in range(cols_n):
            h, q = divmod(c, rows_n)
            pairs.append((r * cols_n + c, q * cols_n + h * rows_n + r))
    return lax.ppermute(value, ("row", "col"), pairs)


def gather_col(piece):
    cols_n = lax.axis_size("col")
    got = {0: piece}
    for m in sorted(range(2, cols_n, 2), reverse=True):
        got[m] = exchange(piece, "col", m)
    got[1] = exchange(piece, "col", 1)
    for m in range(2, cols_n, 2):
        got[m + 1] = exchange(got[m], "col", 1)
    return [got[m] for m in range(cols_n)]


def scatter_col(pieces):
    cols_n = len(pieces)
    order = sorted(range(0, cols_n, 2), reverse=True)
    arrived = {m: exchange(pieces[m + 1], "col", 1) for m in order}
    total = None
    for m in order:
        part = pieces[m] + arrived[m]
        if m:
            part = exchange(part, "col", m)
        total = part if total is None else total + part
    return total


def gather_row(piece):
    rows_n = lax.axis_size("row")
    got = {0: piece}
    mask = rows_n // 2
    while mask:
        for m in list(got):
            got[m + mask] = exchange(got[m], "row", mask)
        mask //= 2
    return [got[m] for m in range(rows_n)]


def scatter_row(pieces):
    rows_n = len(pieces)
    held = dict(enumerate(pieces))
    mask = 1
    while mask < rows_n:
        sent = {m: exchange(held[m], "row", mask) for m in held if m & mask}
        held = {m: held[m] + sent[m | mask] for m in held if not m & mask}
        mask *= 2
    return held[0]


def sum_over(value, axes):
    cols_n = lax.axis_size("col")
    col_bits = [("col", 1 << b) for b in range(cols_n.bit_length() - 1)]
    row_bits = [("row", 1 << b) for b in range(lax.axis_size("row").bit_length() - 1)]
    if axes == "col":
        stages = [col_bits[:1], *[col_bits[b : b + 2] for b in range(1, len(col_bits), 2)]]
    else:
        rest = [col_bits[0], *row_bits[1:], *col_bits[1:]]
        stages = [row_bits[:1], *[rest[b : b + 2] for b in range(0, len(rest), 2)]]
    devices = cols_n * lax.axis_size("row")

    def send(bits):
        mask = sum(size * (cols_n if axis == "row" else 1) for axis, size in bits)
        pairs = [(source, source ^ mask) for source in range(devices)]
        return lax.ppermute(value, ("row", "col"), pairs)

    for bits in stages:
        if len(bits) == 1:
            value = value + send(bits)
        else:
            near, far = send(bits[:1]), send(bits[1:])
            value = (value + near) + (far + send(bits))
    return value


def gram(left_side, right_side):
    return jnp.einsum(
        "nk,nl->kl", left_side, right_side, precision=HIGHEST, preferred_element_type=F32
    )


def mix(vectors, matrix):
    return jnp.dot(vectors, matrix, precision=HIGHEST, preferred_element_type=F32)


def split(value):
    high = value.astype(BF16)
    return high, (value - high.astype(F32)).astype(BF16)


def dot(left_side, right_side):
    return jnp.dot(left_side, right_side, preferred_element_type=F32)


class Shape:
    def __init__(self, stored, rhs, rows_n, cols_n):
        self.rows_n, self.cols_n = rows_n, cols_n
        self.groups = cols_n // rows_n
        self.bs = stored.shape[2]
        self.col_blocks = stored.shape[3]
        self.k = rhs.shape[-1]
        self.per = 2 if self.col_blocks % 2 == 0 else 1
        self.tile = self.per * self.bs
        self.n = self.col_blocks // self.per
        self.odd = self.n % 2
        self.pairs = (self.n + self.odd) // 2
        self.width = (self.n + 1 - self.odd) * self.tile
        self.colset = self.col_blocks * self.bs
        self.unit = self.colset // rows_n

    def strips(self, pair):
        out = [(self.n - 1 - pair, 0, self.n - pair)]
        if pair - self.odd >= 0:
            out.append((pair - self.odd, self.n - pair, pair - self.odd + 1))
        return out


def pack_kernel(sh, index_ref, diag_ref, long_ref, short_ref, hi_ref, lo_ref):
    pair = pl.program_id(0)
    blocks, bs = sh.col_blocks, sh.bs

    def tile(source, tile_col, out_tile, on_diag):
        for a in range(sh.per):
            for b in range(sh.per):
                rows = slice(a * bs, (a + 1) * bs)
                cols = pl.ds(pl.multiple_of(out_tile * sh.tile + b * bs, bs), bs)
                if on_diag and a < b:
                    hi_ref[rows, cols] = jnp.zeros((bs, bs), BF16)
                    lo_ref[rows, cols] = jnp.zeros((bs, bs), BF16)
                    continue
                block = source[a, pl.ds(tile_col * sh.per + b, bs, stride=blocks), :]
                if on_diag and a == b:
                    block = block * diag_ref[0]
                high, low = split(block)
                hi_ref[rows, cols] = high
                lo_ref[rows, cols] = low

    def strip(source, tile_row, first):
        def step(j, carry):
            tile(source, j, first + j, False)
            return carry

        lax.fori_loop(0, tile_row, step, 0)
        tile(source, tile_row, first + tile_row, True)

    strip(long_ref, sh.n - 1 - pair, 0)
    if sh.odd:
        @pl.when(pair >= 1)
        def _():
            strip(short_ref, pair - 1, sh.n - pair)
    else:
        strip(short_ref, pair, sh.n - pair)


def pack(sh, index, stored, diag, group):
    view = stored.reshape(sh.col_blocks, sh.groups, sh.bs * sh.col_blocks, sh.bs)
    block = (sh.per, None, sh.bs * sh.col_blocks, sh.bs)
    out_block = (None, sh.tile, sh.width)
    shape = jax.ShapeDtypeStruct((sh.pairs, sh.tile, sh.width), BF16)
    size = sh.pairs * sh.tile * sh.width

    def long_map(q, index_ref):
        return (sh.n - 1 - q, index_ref[2] ^ group, 0, 0)

    def short_map(q, index_ref):
        return (jnp.maximum(q - sh.odd, 0), index_ref[2] ^ group, 0, 0)

    return pl.pallas_call(
        functools.partial(pack_kernel, sh),
        grid_spec=pltpu.PrefetchScalarGridSpec(
            num_scalar_prefetch=1,
            grid=(sh.pairs,),
            in_specs=[SCALARS, pl.BlockSpec(block, long_map), pl.BlockSpec(block, short_map)],
            out_specs=[pl.BlockSpec(out_block, lambda q, index_ref: (q, 0, 0))] * 2,
        ),
        out_shape=[shape, shape],
        compiler_params=params(),
        cost_estimate=pl.CostEstimate(flops=40 * size, bytes_accessed=12 * size, transcendentals=0),
        name="pack_lower",
    )(index, diag, view, view)


def combined(first, second, weights):
    k = first.shape[-1]
    high, low = split(jnp.concatenate([first, second], axis=1))
    both = dot(high, weights[...]) + dot(low, weights[...])
    return both[:, :k] + both[:, k:]


def unit_rows(sh, position):
    return pl.ds(pl.multiple_of(position * sh.unit, 8), sh.unit)


def halves_kernel(sh, mixing, *refs):
    refs = list(refs)
    index_ref, start_ref = refs.pop(0), refs.pop(0)
    if mixing:
        image_refs, weight_ref = refs[: sh.rows_n], refs[sh.rows_n]
        halves, vector_ref = refs[sh.rows_n + 1 :]
        for m, image in enumerate(image_refs):
            where = unit_rows(sh, index_ref[0] ^ m)
            vector_ref[where, :] = combined(start_ref[where, :], image[...], weight_ref)
        source = vector_ref
    else:
        (halves,) = refs
        source = start_ref
    high, low = split(source[...])
    halves[:, : sh.k] = high
    halves[:, sh.k :] = low


def column_halves(sh, index, start, images=None, weights=None):
    mixing = images is not None
    outs = [jax.ShapeDtypeStruct((sh.colset, 2 * sh.k), BF16)]
    extra = []
    if mixing:
        outs.append(jax.ShapeDtypeStruct((sh.colset, sh.k), F32))
        extra = [*images, weights]
    got = pl.pallas_call(
        functools.partial(halves_kernel, sh, mixing),
        in_specs=[SCALARS, WHOLE, *[WHOLE] * len(extra)],
        out_specs=[WHOLE] * len(outs),
        out_shape=outs,
        compiler_params=params(),
        name="column_halves",
    )(index, start, *extra)
    return got if mixing else (got[0], start)


def rows_kernel(sh, index_ref, hi_ref, lo_ref, halves, after_ref, *refs):
    out_refs, total = refs[:-1], refs[-1]
    pair = pl.program_id(0)
    k, t = sh.k, sh.tile
    for pair_now in range(sh.pairs):
        @pl.when(pair == pair_now)
        def _():
            for tile_row, first, count in sh.strips(pair_now):
                cols = slice(first * t, (first + count) * t)
                both = dot(hi_ref[:, cols], halves[: count * t, :])
                both += dot(lo_ref[:, cols], halves[: count * t, :])
                total[tile_row * t : (tile_row + 1) * t, :] = both[:, :k] + both[:, k:]

    @pl.when(pair == sh.pairs - 1)
    def _():
        for m, out in enumerate(out_refs):
            out[...] = total[unit_rows(sh, index_ref[3] ^ m), :]


def packed_specs(sh):
    return [pl.BlockSpec((None, sh.tile, sh.width), lambda q: (q, 0, 0))] * 2


def product_cost(sh):
    size = sh.pairs * sh.tile * sh.width
    return pl.CostEstimate(flops=40 * size * sh.k, bytes_accessed=4 * size, transcendentals=0)


def apply_rows(sh, index, packed, halves, after):
    piece = jax.ShapeDtypeStruct((sh.unit, sh.k), F32)
    return pl.pallas_call(
        functools.partial(rows_kernel, sh),
        grid=(sh.pairs,),
        in_specs=[SCALARS, *packed_specs(sh), WHOLE, pl.BlockSpec(memory_space=pl.ANY)],
        out_specs=[WHOLE] * sh.rows_n,
        out_shape=[piece] * sh.rows_n,
        scratch_shapes=[pltpu.VMEM((sh.colset, sh.k), F32)],
        compiler_params=params(),
        cost_estimate=product_cost(sh),
        name="lower_times",
    )(index, *packed, halves, after)


def cols_kernel(sh, mixing, first_call, last_call, *refs):
    refs = list(refs)
    index_ref, hi_ref, lo_ref = refs[:3]
    del refs[:3]
    start_refs = [refs.pop(0) for _ in range(sh.rows_n)]
    image_refs = [refs.pop(0) for _ in range(sh.rows_n)] if mixing else []
    weight_ref = refs.pop(0) if mixing else None
    before_ref = None if first_call else refs.pop(0)
    column_ref = refs.pop(0) if last_call else None
    refs.pop(0)
    if last_call:
        out_refs = [refs.pop(0) for _ in range(sh.rows_n)]
        curve_ref = refs.pop(0)
        vector, total, turned = refs
    else:
        total, vector = refs
    pair = pl.program_id(0)
    k, t = sh.k, sh.tile

    @pl.when(pair == 0)
    def _():
        for m in range(sh.rows_n):
            where = unit_rows(sh, index_ref[3] ^ m)
            if mixing:
                vector[where, :] = combined(start_refs[m][...], image_refs[m][...], weight_ref)
            else:
                vector[where, :] = start_refs[m][...]
        total[...] = jnp.zeros_like(total) if first_call else before_ref[...]

    for pair_now in range(sh.pairs):
        @pl.when(pair == pair_now)
        def _():
            for tile_row, first, count in sh.strips(pair_now):
                high, low = split(vector[tile_row * t : (tile_row + 1) * t, :].T)
                stacked = jnp.concatenate([high, low], axis=0)
                for j in range(count):
                    cols = slice((first + j) * t, (first + j + 1) * t)
                    both = dot(stacked, hi_ref[:, cols]) + dot(stacked, lo_ref[:, cols])
                    total[:, j * t : (j + 1) * t] += both[:k] + both[k:]

    if last_call:
        @pl.when(pair == sh.pairs - 1)
        def _():
            turned[...] = total[...].T
            for m, out in enumerate(out_refs):
                out[...] = turned[unit_rows(sh, index_ref[0] ^ m), :]
            curve_ref[...] = jnp.dot(
                total[...], column_ref[...], precision=HIGHEST, preferred_element_type=F32
            )


def apply_cols(sh, index, packed, starts, after, images=(), weights=None, before=None, column=None):
    mixing, last_call = bool(images), column is not None
    operands = [*starts, *images]
    operands += [value for value in (weights, before, column) if value is not None]
    piece = jax.ShapeDtypeStruct((sh.unit, sh.k), F32)
    sums = (sh.k, sh.colset)
    vector = pltpu.VMEM((sh.colset, sh.k), F32)
    if last_call:
        outs = [piece] * sh.rows_n + [jax.ShapeDtypeStruct((sh.k, sh.k), F32)]
        scratch = [vector, pltpu.VMEM(sums, F32), vector]
    else:
        outs = [jax.ShapeDtypeStruct(sums, F32)]
        scratch = [vector]
    got = pl.pallas_call(
        functools.partial(cols_kernel, sh, mixing, before is None, last_call),
        grid=(sh.pairs,),
        in_specs=[
            SCALARS,
            *packed_specs(sh),
            *[WHOLE] * len(operands),
            pl.BlockSpec(memory_space=pl.ANY),
        ],
        out_specs=[WHOLE] * len(outs),
        out_shape=outs,
        scratch_shapes=scratch,
        compiler_params=params(),
        cost_estimate=product_cost(sh),
        name="upper_times",
    )(index, *packed, *operands, after)
    return (got[: sh.rows_n], got[sh.rows_n]) if last_call else got[0]


def solve_kernel(symmetric, panel, matrix_ref, target_ref, out_ref):
    size = matrix_ref.shape[0]
    matrix, target = matrix_ref[...], target_ref[...]
    if not symmetric:
        matrix = matrix + matrix.T
    rows = lax.broadcasted_iota(jnp.int32, (size, size), 0)
    for first in range(0, size, panel):
        spread = [
            jnp.broadcast_to(matrix[:, first + i : first + i + 1], (size, size))
            for i in range(panel)
        ]
        for i in range(panel):
            pivot = slice(first + i, first + i + 1)
            here, column = rows == first + i, spread[i]
            inverse = 1.0 / column[pivot, :]

            def eliminate(value):
                scaled = value[pivot, :] * inverse
                return jnp.where(here, scaled, value - column * scaled)

            for later in range(i + 1, panel):
                spread[later] = eliminate(spread[later])
            matrix, target = eliminate(matrix), eliminate(target)
    out_ref[...] = target


def solve(matrix, target, symmetric):
    return pl.pallas_call(
        functools.partial(solve_kernel, symmetric, 8),
        in_specs=[WHOLE, WHOLE],
        out_specs=WHOLE,
        out_shape=jax.ShapeDtypeStruct(target.shape, F32),
        cost_estimate=pl.CostEstimate(
            flops=1 << 32, bytes_accessed=1 << 17, transcendentals=0
        ),
        name="solve_spd",
    )(matrix, target)


def weights_kernel(inverse_ref, gram_ref, step_ref, out_ref):
    k = step_ref.shape[-1]
    mixed = jnp.dot(
        inverse_ref[...], gram_ref[...], precision=HIGHEST, preferred_element_type=F32
    )
    rows = lax.broadcasted_iota(jnp.int32, (k, k), 0)
    cols = lax.broadcasted_iota(jnp.int32, (k, k), 1)
    mixed = jnp.where(rows == cols, mixed + 1.0, mixed)
    for base, value in ((0, mixed), (k, -step_ref[...])):
        high, low = split(value)
        out_ref[base : base + k, :k] = high
        out_ref[base : base + k, k:] = low


def next_weights(inverse, gram_next, step_size):
    k = step_size.shape[-1]
    return pl.pallas_call(
        weights_kernel,
        in_specs=[WHOLE] * 3,
        out_specs=WHOLE,
        out_shape=jax.ShapeDtypeStruct((2 * k, 2 * k), BF16),
        name="next_weights",
    )(inverse, gram_next, step_size)


def order_kernel(sh, index_ref, *refs):
    out_ref = refs[-1]
    for m, piece in enumerate(refs[:-1]):
        out_ref[unit_rows(sh, index_ref[0] ^ m), :] = piece[...]


def in_order(sh, index, pieces):
    return pl.pallas_call(
        functools.partial(order_kernel, sh),
        in_specs=[SCALARS, *[WHOLE] * len(pieces)],
        out_specs=WHOLE,
        out_shape=jax.ShapeDtypeStruct((sh.colset, sh.k), F32),
        compiler_params=params(),
        name="in_order",
    )(index, *pieces)


def image_parts(sh, index, packed, halves, column, starts, images=None, weights=None):
    n = sh.rows_n
    row_parts = [None] * sh.groups
    after = halves
    for group in reversed(range(sh.groups)):
        row_parts[group] = apply_rows(sh, index, packed[group], halves, after)
        after = row_parts[group][0]
    before = None
    for group in range(sh.groups):
        last = group == sh.groups - 1
        near = slice(group * n, (group + 1) * n)
        before = apply_cols(
            sh,
            index,
            packed[group],
            starts[near],
            after,
            images=images[near] if images else (),
            weights=weights,
            before=before,
            column=column if last else None,
        )
    return [part for parts in row_parts for part in parts], *before


def steps(stored, rhs):
    row_index = lax.axis_index("row")
    col_index = lax.axis_index("col")
    rows_n = lax.axis_size("row")
    cols_n = lax.axis_size("col")
    sh = Shape(stored, rhs, rows_n, cols_n)
    groups = range(sh.groups)
    own_group = col_index // rows_n
    index = jnp.stack([row_index, col_index, own_group, col_index % rows_n]).astype(jnp.int32)

    def diag_of(group):
        offset = (own_group ^ group) * rows_n + row_index - col_index
        weight = jnp.where(offset > 0, 1.0, jnp.where(offset == 0, 0.5, 0.0))
        return weight.astype(F32).reshape(1)

    start = rhs.reshape(sh.colset, sh.k)
    start_piece = lax.dynamic_slice_in_dim(start, row_index * sh.unit, sh.unit, 0)
    start_rows = gather_col(swap(start_piece))
    packed = [pack(sh, index, stored, diag_of(group), group) for group in groups]
    halves, _ = column_halves(sh, index, start)
    gram_now = sum_over(gram(start, start), "col")
    inverse = solve(gram_now, jnp.eye(sh.k, dtype=F32), True)

    row_parts, col_parts, curve = image_parts(sh, index, packed, halves, start, start_rows)
    row_piece = scatter_col(row_parts)
    curve = sum_over(curve, "all")
    step_size = solve(curve, gram_now, False)
    col_piece = scatter_row(col_parts)
    image_far = row_piece + swap(col_piece)
    image_piece = col_piece + swap(row_piece)
    image_rows = gather_col(image_far)
    image_cols = gather_row(image_piece)
    residual_piece = start_piece - mix(image_piece, step_size)
    gram_next = sum_over(gram(residual_piece, residual_piece), "all")

    weights = next_weights(inverse, gram_next, step_size)
    halves, direction = column_halves(sh, index, start, image_cols, weights)
    row_parts, col_parts, curve = image_parts(
        sh, index, packed, halves, direction, start_rows, image_rows, weights
    )
    row_piece = scatter_col(row_parts)
    curve = sum_over(curve, "all")
    last_step = solve(curve, gram_next, False)
    answer = mix(start, step_size) + mix(direction, last_step)
    image_piece = scatter_row(col_parts) + swap(row_piece)
    residual_piece = residual_piece - mix(image_piece, last_step)
    residual = in_order(sh, index, gather_row(residual_piece))
    return answer.reshape(rhs.shape), residual.reshape(rhs.shape)


def solution(mesh):
    placed = (P(None, "row", None, None, "col", None), P(None, "col", None, None))
    return jax.shard_map(
        steps,
        mesh=mesh,
        in_specs=placed,
        out_specs=(P(None, "col", None, None), P(None, "col", None, None)),
        check_vma=False,
    )
```

```python
import functools

import jax
import jax.numpy as jnp
from jax import lax
from jax.experimental import pallas as pl
from jax.experimental.pallas import tpu as pltpu
from jax.sharding import PartitionSpec as P


HIGHEST = lax.Precision.HIGHEST
F32 = jnp.float32
BF16 = jnp.bfloat16
WHOLE = pl.BlockSpec(memory_space=pltpu.VMEM)
SCALARS = pl.BlockSpec(memory_space=pltpu.SMEM)


def params(limit=60 * 1024 * 1024):
    return pltpu.CompilerParams(vmem_limit_bytes=limit)


def exchange(value, axis, mask):
    pairs = [(source, source ^ mask) for source in range(lax.axis_size(axis))]
    return lax.ppermute(value, axis, pairs)


def swap(value):
    rows_n = lax.axis_size("row")
    cols_n = lax.axis_size("col")
    pairs = []
    for r in range(rows_n):
        for c in range(cols_n):
            h, q = divmod(c, rows_n)
            pairs.append((r * cols_n + c, q * cols_n + h * rows_n + r))
    return lax.ppermute(value, ("row", "col"), pairs)


def gather_col(piece):
    cols_n = lax.axis_size("col")
    got = {0: piece}
    for m in sorted(range(2, cols_n, 2), reverse=True):
        got[m] = exchange(piece, "col", m)
    got[1] = exchange(piece, "col", 1)
    for m in range(2, cols_n, 2):
        got[m + 1] = exchange(got[m], "col", 1)
    return [got[m] for m in range(cols_n)]


def scatter_col(pieces):
    cols_n = len(pieces)
    order = sorted(range(0, cols_n, 2), reverse=True)
    arrived = {m: exchange(pieces[m + 1], "col", 1) for m in order}
    total = None
    for m in order:
        part = pieces[m] + arrived[m]
        if m:
            part = exchange(part, "col", m)
        total = part if total is None else total + part
    return total


def gather_row(piece):
    rows_n = lax.axis_size("row")
    got = {0: piece}
    mask = rows_n // 2
    while mask:
        for m in list(got):
            got[m + mask] = exchange(got[m], "row", mask)
        mask //= 2
    return [got[m] for m in range(rows_n)]


def scatter_row(pieces):
    rows_n = len(pieces)
    held = dict(enumerate(pieces))
    mask = 1
    while mask < rows_n:
        sent = {m: exchange(held[m], "row", mask) for m in held if m & mask}
        held = {m: held[m] + sent[m | mask] for m in held if not m & mask}
        mask *= 2
    return held[0]


def sum_over(value, axes):
    cols_n = lax.axis_size("col")
    col_bits = [("col", 1 << b) for b in range(cols_n.bit_length() - 1)]
    row_bits = [("row", 1 << b) for b in range(lax.axis_size("row").bit_length() - 1)]
    if axes == "col":
        stages = [col_bits[:1], *[col_bits[b : b + 2] for b in range(1, len(col_bits), 2)]]
    else:
        rest = [col_bits[0], *row_bits[1:], *col_bits[1:]]
        stages = [row_bits[:1], *[rest[b : b + 2] for b in range(0, len(rest), 2)]]
    devices = cols_n * lax.axis_size("row")

    def send(bits):
        mask = sum(size * (cols_n if axis == "row" else 1) for axis, size in bits)
        pairs = [(source, source ^ mask) for source in range(devices)]
        return lax.ppermute(value, ("row", "col"), pairs)

    for bits in stages:
        if len(bits) == 1:
            value = value + send(bits)
        else:
            near, far = send(bits[:1]), send(bits[1:])
            value = (value + near) + (far + send(bits))
    return value


def gram(left_side, right_side):
    return jnp.einsum(
        "nk,nl->kl", left_side, right_side, precision=HIGHEST, preferred_element_type=F32
    )


def mix(vectors, matrix):
    return jnp.dot(vectors, matrix, precision=HIGHEST, preferred_element_type=F32)


def split(value):
    high = value.astype(BF16)
    return high, (value - high.astype(F32)).astype(BF16)


def dot(left_side, right_side):
    return jnp.dot(left_side, right_side, preferred_element_type=F32)


class Shape:
    def __init__(self, stored, rhs, rows_n, cols_n):
        self.rows_n, self.cols_n = rows_n, cols_n
        self.groups = cols_n // rows_n
        self.bs = stored.shape[2]
        self.col_blocks = stored.shape[3]
        self.k = rhs.shape[-1]
        self.per = 2 if self.col_blocks % 2 == 0 else 1
        self.tile = self.per * self.bs
        self.n = self.col_blocks // self.per
        self.odd = self.n % 2
        self.pairs = (self.n + self.odd) // 2
        self.width = (self.n + 1 - self.odd) * self.tile
        self.colset = self.col_blocks * self.bs
        self.unit = self.colset // rows_n

    def strips(self, pair):
        out = [(self.n - 1 - pair, 0, self.n - pair)]
        if pair - self.odd >= 0:
            out.append((pair - self.odd, self.n - pair, pair - self.odd + 1))
        return out


def pack_kernel(sh, index_ref, diag_ref, long_ref, short_ref, hi_ref, lo_ref):
    pair = pl.program_id(0)
    blocks, bs = sh.col_blocks, sh.bs

    def tile(source, tile_col, out_tile, on_diag):
        for a in range(sh.per):
            for b in range(sh.per):
                rows = slice(a * bs, (a + 1) * bs)
                cols = pl.ds(pl.multiple_of(out_tile * sh.tile + b * bs, bs), bs)
                if on_diag and a < b:
                    hi_ref[rows, cols] = jnp.zeros((bs, bs), BF16)
                    lo_ref[rows, cols] = jnp.zeros((bs, bs), BF16)
                    continue
                block = source[a, pl.ds(tile_col * sh.per + b, bs, stride=blocks), :]
                if on_diag and a == b:
                    block = block * diag_ref[0]
                high, low = split(block)
                hi_ref[rows, cols] = high
                lo_ref[rows, cols] = low

    def strip(source, tile_row, first):
        def step(j, carry):
            tile(source, j, first + j, False)
            return carry

        lax.fori_loop(0, tile_row, step, 0)
        tile(source, tile_row, first + tile_row, True)

    strip(long_ref, sh.n - 1 - pair, 0)
    if sh.odd:
        @pl.when(pair >= 1)
        def _():
            strip(short_ref, pair - 1, sh.n - pair)
    else:
        strip(short_ref, pair, sh.n - pair)


def pack(sh, index, stored, diag, group):
    view = stored.reshape(sh.col_blocks, sh.groups, sh.bs * sh.col_blocks, sh.bs)
    block = (sh.per, None, sh.bs * sh.col_blocks, sh.bs)
    out_block = (None, sh.tile, sh.width)
    shape = jax.ShapeDtypeStruct((sh.pairs, sh.tile, sh.width), BF16)
    size = sh.pairs * sh.tile * sh.width

    def long_map(q, index_ref):
        return (sh.n - 1 - q, index_ref[2] ^ group, 0, 0)

    def short_map(q, index_ref):
        return (jnp.maximum(q - sh.odd, 0), index_ref[2] ^ group, 0, 0)

    return pl.pallas_call(
        functools.partial(pack_kernel, sh),
        grid_spec=pltpu.PrefetchScalarGridSpec(
            num_scalar_prefetch=1,
            grid=(sh.pairs,),
            in_specs=[SCALARS, pl.BlockSpec(block, long_map), pl.BlockSpec(block, short_map)],
            out_specs=[pl.BlockSpec(out_block, lambda q, index_ref: (q, 0, 0))] * 2,
        ),
        out_shape=[shape, shape],
        compiler_params=params(),
        cost_estimate=pl.CostEstimate(flops=40 * size, bytes_accessed=12 * size, transcendentals=0),
        name="pack_lower",
    )(index, diag, view, view)


def combined(first, second, weights):
    k = first.shape[-1]
    high, low = split(jnp.concatenate([first, second], axis=1))
    both = dot(high, weights[...]) + dot(low, weights[...])
    return both[:, :k] + both[:, k:]


def unit_rows(sh, position):
    return pl.ds(pl.multiple_of(position * sh.unit, 8), sh.unit)


def halves_kernel(sh, mixing, *refs):
    refs = list(refs)
    index_ref, start_ref = refs.pop(0), refs.pop(0)
    if mixing:
        image_refs, weight_ref = refs[: sh.rows_n], refs[sh.rows_n]
        halves, vector_ref = refs[sh.rows_n + 1 :]
        for m, image in enumerate(image_refs):
            where = unit_rows(sh, index_ref[0] ^ m)
            vector_ref[where, :] = combined(start_ref[where, :], image[...], weight_ref)
        source = vector_ref
    else:
        (halves,) = refs
        source = start_ref
    high, low = split(source[...])
    halves[:, : sh.k] = high
    halves[:, sh.k :] = low


def column_halves(sh, index, start, images=None, weights=None):
    mixing = images is not None
    outs = [jax.ShapeDtypeStruct((sh.colset, 2 * sh.k), BF16)]
    extra = []
    if mixing:
        outs.append(jax.ShapeDtypeStruct((sh.colset, sh.k), F32))
        extra = [*images, weights]
    got = pl.pallas_call(
        functools.partial(halves_kernel, sh, mixing),
        in_specs=[SCALARS, WHOLE, *[WHOLE] * len(extra)],
        out_specs=[WHOLE] * len(outs),
        out_shape=outs,
        compiler_params=params(),
        name="column_halves",
    )(index, start, *extra)
    return got if mixing else (got[0], start)


def rows_kernel(sh, index_ref, hi_ref, lo_ref, halves, after_ref, *refs):
    out_refs, total = refs[:-1], refs[-1]
    pair = pl.program_id(0)
    k, t = sh.k, sh.tile
    for pair_now in range(sh.pairs):
        @pl.when(pair == pair_now)
        def _():
            for tile_row, first, count in sh.strips(pair_now):
                cols = slice(first * t, (first + count) * t)
                both = dot(hi_ref[:, cols], halves[: count * t, :])
                both += dot(lo_ref[:, cols], halves[: count * t, :])
                total[tile_row * t : (tile_row + 1) * t, :] = both[:, :k] + both[:, k:]

    @pl.when(pair == sh.pairs - 1)
    def _():
        for m, out in enumerate(out_refs):
            out[...] = total[unit_rows(sh, index_ref[3] ^ m), :]


def packed_specs(sh):
    return [pl.BlockSpec((None, sh.tile, sh.width), lambda q: (q, 0, 0))] * 2


def product_cost(sh):
    size = sh.pairs * sh.tile * sh.width
    return pl.CostEstimate(flops=40 * size * sh.k, bytes_accessed=4 * size, transcendentals=0)


def apply_rows(sh, index, packed, halves, after):
    piece = jax.ShapeDtypeStruct((sh.unit, sh.k), F32)
    return pl.pallas_call(
        functools.partial(rows_kernel, sh),
        grid=(sh.pairs,),
        in_specs=[SCALARS, *packed_specs(sh), WHOLE, pl.BlockSpec(memory_space=pl.ANY)],
        out_specs=[WHOLE] * sh.rows_n,
        out_shape=[piece] * sh.rows_n,
        scratch_shapes=[pltpu.VMEM((sh.colset, sh.k), F32)],
        compiler_params=params(),
        cost_estimate=product_cost(sh),
        name="lower_times",
    )(index, *packed, halves, after)


def cols_kernel(sh, mixing, first_call, last_call, *refs):
    refs = list(refs)
    index_ref, hi_ref, lo_ref = refs[:3]
    del refs[:3]
    start_refs = [refs.pop(0) for _ in range(sh.rows_n)]
    image_refs = [refs.pop(0) for _ in range(sh.rows_n)] if mixing else []
    weight_ref = refs.pop(0) if mixing else None
    before_ref = None if first_call else refs.pop(0)
    column_ref = refs.pop(0) if last_call else None
    refs.pop(0)
    if last_call:
        out_refs = [refs.pop(0) for _ in range(sh.rows_n)]
        curve_ref = refs.pop(0)
        vector, total, turned = refs
    else:
        total, vector = refs
    pair = pl.program_id(0)
    k, t = sh.k, sh.tile

    @pl.when(pair == 0)
    def _():
        for m in range(sh.rows_n):
            where = unit_rows(sh, index_ref[3] ^ m)
            if mixing:
                vector[where, :] = combined(start_refs[m][...], image_refs[m][...], weight_ref)
            else:
                vector[where, :] = start_refs[m][...]
        total[...] = jnp.zeros_like(total) if first_call else before_ref[...]

    for pair_now in range(sh.pairs):
        @pl.when(pair == pair_now)
        def _():
            for tile_row, first, count in sh.strips(pair_now):
                high, low = split(vector[tile_row * t : (tile_row + 1) * t, :].T)
                stacked = jnp.concatenate([high, low], axis=0)
                for j in range(count):
                    cols = slice((first + j) * t, (first + j + 1) * t)
                    both = dot(stacked, hi_ref[:, cols]) + dot(stacked, lo_ref[:, cols])
                    total[:, j * t : (j + 1) * t] += both[:k] + both[k:]

    if last_call:
        @pl.when(pair == sh.pairs - 1)
        def _():
            turned[...] = total[...].T
            for m, out in enumerate(out_refs):
                out[...] = turned[unit_rows(sh, index_ref[0] ^ m), :]
            curve_ref[...] = jnp.dot(
                total[...], column_ref[...], precision=HIGHEST, preferred_element_type=F32
            )


def apply_cols(sh, index, packed, starts, after, images=(), weights=None, before=None, column=None):
    mixing, last_call = bool(images), column is not None
    operands = [*starts, *images]
    operands += [value for value in (weights, before, column) if value is not None]
    piece = jax.ShapeDtypeStruct((sh.unit, sh.k), F32)
    sums = (sh.k, sh.colset)
    vector = pltpu.VMEM((sh.colset, sh.k), F32)
    if last_call:
        outs = [piece] * sh.rows_n + [jax.ShapeDtypeStruct((sh.k, sh.k), F32)]
        scratch = [vector, pltpu.VMEM(sums, F32), vector]
    else:
        outs = [jax.ShapeDtypeStruct(sums, F32)]
        scratch = [vector]
    got = pl.pallas_call(
        functools.partial(cols_kernel, sh, mixing, before is None, last_call),
        grid=(sh.pairs,),
        in_specs=[
            SCALARS,
            *packed_specs(sh),
            *[WHOLE] * len(operands),
            pl.BlockSpec(memory_space=pl.ANY),
        ],
        out_specs=[WHOLE] * len(outs),
        out_shape=outs,
        scratch_shapes=scratch,
        compiler_params=params(),
        cost_estimate=product_cost(sh),
        name="upper_times",
    )(index, *packed, *operands, after)
    return (got[: sh.rows_n], got[sh.rows_n]) if last_call else got[0]


def solve_kernel(symmetric, panel, matrix_ref, target_ref, out_ref):
    size = matrix_ref.shape[0]
    matrix, target = matrix_ref[...], target_ref[...]
    if not symmetric:
        matrix = matrix + matrix.T
    rows = lax.broadcasted_iota(jnp.int32, (size, size), 0)
    for first in range(0, size, panel):
        spread = [
            jnp.broadcast_to(matrix[:, first + i : first + i + 1], (size, size))
            for i in range(panel)
        ]
        for i in range(panel):
            pivot = slice(first + i, first + i + 1)
            here, column = rows == first + i, spread[i]
            inverse = 1.0 / column[pivot, :]

            def eliminate(value):
                scaled = value[pivot, :] * inverse
                return jnp.where(here, scaled, value - column * scaled)

            for later in range(i + 1, panel):
                spread[later] = eliminate(spread[later])
            matrix, target = eliminate(matrix), eliminate(target)
    out_ref[...] = target


def solve(matrix, target, symmetric):
    return pl.pallas_call(
        functools.partial(solve_kernel, symmetric, 8),
        in_specs=[WHOLE, WHOLE],
        out_specs=WHOLE,
        out_shape=jax.ShapeDtypeStruct(target.shape, F32),
        cost_estimate=pl.CostEstimate(
            flops=1 << 32, bytes_accessed=1 << 17, transcendentals=0
        ),
        name="solve_spd",
    )(matrix, target)


def weights_kernel(inverse_ref, gram_ref, step_ref, out_ref):
    k = step_ref.shape[-1]
    mixed = jnp.dot(
        inverse_ref[...], gram_ref[...], precision=HIGHEST, preferred_element_type=F32
    )
    rows = lax.broadcasted_iota(jnp.int32, (k, k), 0)
    cols = lax.broadcasted_iota(jnp.int32, (k, k), 1)
    mixed = jnp.where(rows == cols, mixed + 1.0, mixed)
    for base, value in ((0, mixed), (k, -step_ref[...])):
        high, low = split(value)
        out_ref[base : base + k, :k] = high
        out_ref[base : base + k, k:] = low


def next_weights(inverse, gram_next, step_size):
    k = step_size.shape[-1]
    return pl.pallas_call(
        weights_kernel,
        in_specs=[WHOLE] * 3,
        out_specs=WHOLE,
        out_shape=jax.ShapeDtypeStruct((2 * k, 2 * k), BF16),
        name="next_weights",
    )(inverse, gram_next, step_size)


def answer_kernel(start_ref, direction_ref, step_ref, last_ref, out_ref):
    def part(vectors, matrix):
        return jnp.dot(vectors, matrix, precision=HIGHEST, preferred_element_type=F32)

    out_ref[...] = part(start_ref[...], step_ref[...]) + part(direction_ref[...], last_ref[...])


def answer_of(sh, start, direction, step_size, last_step):
    strip = pl.BlockSpec((sh.tile, sh.k), lambda i: (i, 0))
    return pl.pallas_call(
        answer_kernel,
        grid=(sh.n,),
        in_specs=[strip, strip, WHOLE, WHOLE],
        out_specs=strip,
        out_shape=jax.ShapeDtypeStruct((sh.colset, sh.k), F32),
        name="answer",
    )(start, direction, step_size, last_step)


def order_kernel(sh, index_ref, *refs):
    out_ref = refs[-1]
    for m, piece in enumerate(refs[:-1]):
        out_ref[unit_rows(sh, index_ref[0] ^ m), :] = piece[...]


def in_order(sh, index, pieces):
    return pl.pallas_call(
        functools.partial(order_kernel, sh),
        in_specs=[SCALARS, *[WHOLE] * len(pieces)],
        out_specs=WHOLE,
        out_shape=jax.ShapeDtypeStruct((sh.colset, sh.k), F32),
        compiler_params=params(),
        name="in_order",
    )(index, *pieces)


def image_parts(sh, index, packed, halves, column, starts, images=None, weights=None):
    n = sh.rows_n
    row_parts = [None] * sh.groups
    after = halves
    for group in reversed(range(sh.groups)):
        row_parts[group] = apply_rows(sh, index, packed[group], halves, after)
        after = row_parts[group][0]
    before = None
    for group in range(sh.groups):
        last = group == sh.groups - 1
        near = slice(group * n, (group + 1) * n)
        before = apply_cols(
            sh,
            index,
            packed[group],
            starts[near],
            after,
            images=images[near] if images else (),
            weights=weights,
            before=before,
            column=column if last else None,
        )
    return [part for parts in row_parts for part in parts], *before


def steps(stored, rhs):
    row_index = lax.axis_index("row")
    col_index = lax.axis_index("col")
    rows_n = lax.axis_size("row")
    cols_n = lax.axis_size("col")
    sh = Shape(stored, rhs, rows_n, cols_n)
    groups = range(sh.groups)
    own_group = col_index // rows_n
    index = jnp.stack([row_index, col_index, own_group, col_index % rows_n]).astype(jnp.int32)

    def diag_of(group):
        offset = (own_group ^ group) * rows_n + row_index - col_index
        weight = jnp.where(offset > 0, 1.0, jnp.where(offset == 0, 0.5, 0.0))
        return weight.astype(F32).reshape(1)

    start = rhs.reshape(sh.colset, sh.k)
    start_piece = lax.dynamic_slice_in_dim(start, row_index * sh.unit, sh.unit, 0)
    start_rows = gather_col(swap(start_piece))
    packed = [pack(sh, index, stored, diag_of(group), group) for group in groups]
    halves, _ = column_halves(sh, index, start)
    gram_now = sum_over(gram(start, start), "col")
    inverse = solve(gram_now, jnp.eye(sh.k, dtype=F32), True)

    row_parts, col_parts, curve = image_parts(sh, index, packed, halves, start, start_rows)
    row_piece = scatter_col(row_parts)
    curve = sum_over(curve, "all")
    step_size = solve(curve, gram_now, False)
    col_piece = scatter_row(col_parts)
    image_far = row_piece + swap(col_piece)
    image_piece = col_piece + swap(row_piece)
    image_rows = gather_col(image_far)
    image_cols = gather_row(image_piece)
    residual_piece = start_piece - mix(image_piece, step_size)
    gram_next = sum_over(gram(residual_piece, residual_piece), "all")

    weights = next_weights(inverse, gram_next, step_size)
    halves, direction = column_halves(sh, index, start, image_cols, weights)
    row_parts, col_parts, curve = image_parts(
        sh, index, packed, halves, direction, start_rows, image_rows, weights
    )
    row_piece = scatter_col(row_parts)
    curve = sum_over(curve, "all")
    last_step = solve(curve, gram_next, False)
    answer = answer_of(sh, start, direction, step_size, last_step)
    image_piece = scatter_row(col_parts) + swap(row_piece)
    residual_piece = residual_piece - mix(image_piece, last_step)
    residual = in_order(sh, index, gather_row(residual_piece))
    return answer.reshape(rhs.shape), residual.reshape(rhs.shape)


def solution(mesh):
    placed = (P(None, "row", None, None, "col", None), P(None, "col", None, None))
    return jax.shard_map(
        steps,
        mesh=mesh,
        in_specs=placed,
        out_specs=(P(None, "col", None, None), P(None, "col", None, None)),
        check_vma=False,
    )
```

```python
import functools

import jax
import jax.numpy as jnp
from jax import lax
from jax.experimental import pallas as pl
from jax.experimental.pallas import tpu as pltpu
from jax.sharding import PartitionSpec as P


HIGHEST = lax.Precision.HIGHEST
F32 = jnp.float32
BF16 = jnp.bfloat16
WHOLE = pl.BlockSpec(memory_space=pltpu.VMEM)
SCALARS = pl.BlockSpec(memory_space=pltpu.SMEM)
ANYWHERE = pl.BlockSpec(memory_space=pl.ANY)


def params(mebibytes=8):
    return pltpu.CompilerParams(vmem_limit_bytes=mebibytes << 20)


def exchange(value, axis, mask):
    pairs = [(source, source ^ mask) for source in range(lax.axis_size(axis))]
    return lax.ppermute(value, axis, pairs)


def swap(value):
    rows_n = lax.axis_size("row")
    cols_n = lax.axis_size("col")
    pairs = []
    for r in range(rows_n):
        for c in range(cols_n):
            h, q = divmod(c, rows_n)
            pairs.append((r * cols_n + c, q * cols_n + h * rows_n + r))
    return lax.ppermute(value, ("row", "col"), pairs)


def gather_col(piece):
    cols_n = lax.axis_size("col")
    got = {0: piece}
    for m in sorted(range(2, cols_n, 2), reverse=True):
        got[m] = exchange(piece, "col", m)
    got[1] = exchange(piece, "col", 1)
    for m in range(2, cols_n, 2):
        got[m + 1] = exchange(got[m], "col", 1)
    return [got[m] for m in range(cols_n)]


def scatter_col(pieces):
    cols_n = len(pieces)
    order = sorted(range(0, cols_n, 2), reverse=True)
    arrived = {m: exchange(pieces[m + 1], "col", 1) for m in order}
    total = None
    for m in order:
        part = pieces[m] + arrived[m]
        if m:
            part = exchange(part, "col", m)
        total = part if total is None else total + part
    return total


def gather_row(piece):
    rows_n = lax.axis_size("row")
    got = {0: piece}
    mask = rows_n // 2
    while mask:
        for m in list(got):
            got[m + mask] = exchange(got[m], "row", mask)
        mask //= 2
    return [got[m] for m in range(rows_n)]


def scatter_row(pieces):
    rows_n = len(pieces)
    held = dict(enumerate(pieces))
    mask = 1
    while mask < rows_n:
        sent = {m: exchange(held[m], "row", mask) for m in held if m & mask}
        held = {m: held[m] + sent[m | mask] for m in held if not m & mask}
        mask *= 2
    return held[0]


def sum_over(value, axes):
    cols_n = lax.axis_size("col")
    col_bits = [("col", 1 << b) for b in range(cols_n.bit_length() - 1)]
    row_bits = [("row", 1 << b) for b in range(lax.axis_size("row").bit_length() - 1)]
    if axes == "col":
        stages = [col_bits[:1], *[col_bits[b : b + 2] for b in range(1, len(col_bits), 2)]]
    else:
        rest = [col_bits[0], *row_bits[1:], *col_bits[1:]]
        stages = [row_bits[:1], *[rest[b : b + 2] for b in range(0, len(rest), 2)]]
    devices = cols_n * lax.axis_size("row")

    def send(bits):
        mask = sum(size * (cols_n if axis == "row" else 1) for axis, size in bits)
        pairs = [(source, source ^ mask) for source in range(devices)]
        return lax.ppermute(value, ("row", "col"), pairs)

    for bits in stages:
        if len(bits) == 1:
            value = value + send(bits)
        else:
            near, far = send(bits[:1]), send(bits[1:])
            value = (value + near) + (far + send(bits))
    return value


def gram(left_side, right_side):
    return jnp.einsum(
        "nk,nl->kl", left_side, right_side, precision=HIGHEST, preferred_element_type=F32
    )


def mix(vectors, matrix):
    return jnp.dot(vectors, matrix, precision=HIGHEST, preferred_element_type=F32)


def split(value):
    high = value.astype(BF16)
    return high, (value - high.astype(F32)).astype(BF16)


def dot(left_side, right_side):
    return jnp.dot(left_side, right_side, preferred_element_type=F32)


class Shape:
    def __init__(self, stored, rhs, rows_n, cols_n):
        self.rows_n, self.cols_n = rows_n, cols_n
        self.groups = cols_n // rows_n
        self.bs = stored.shape[2]
        self.col_blocks = stored.shape[3]
        self.k = rhs.shape[-1]
        self.per = 2 if self.col_blocks % 2 == 0 else 1
        self.tile = self.per * self.bs
        self.n = self.col_blocks // self.per
        self.odd = self.n % 2
        self.pairs = (self.n + self.odd) // 2
        self.width = (self.n + 1 - self.odd) * self.tile
        self.colset = self.col_blocks * self.bs
        self.unit = self.colset // rows_n

    def strips(self, pair):
        out = [(self.n - 1 - pair, 0, self.n - pair)]
        if pair - self.odd >= 0:
            out.append((pair - self.odd, self.n - pair, pair - self.odd + 1))
        return out


def pack_kernel(sh, group, index_ref, stored_ref, halves, after_ref, *refs):
    hi_ref, lo_ref = refs[0], refs[1]
    out_refs, (held, total, sems) = refs[2:-3], refs[-3:]
    blocks, bs, t = sh.col_blocks, sh.bs, sh.tile
    strips = [(pair, *strip) for pair in range(sh.pairs) for strip in sh.strips(pair)]
    slots = held.shape[0]
    offset = (index_ref[2] ^ group) * sh.rows_n + index_ref[0] - index_ref[1]
    on_diagonal = jnp.where(offset > 0, 1.0, jnp.where(offset == 0, 0.5, 0.0)).astype(F32)

    def fetch(number):
        tile_row = strips[number][1]
        slot = number % slots
        source = stored_ref.at[pl.ds(tile_row * sh.per, sh.per), index_ref[2] ^ group]
        return pltpu.make_async_copy(source, held.at[slot], sems.at[slot])

    def tile(slot, pair, tile_col, out_tile, on_diag):
        for a in range(sh.per):
            for b in range(sh.per):
                rows = slice(a * bs, (a + 1) * bs)
                cols = pl.ds(pl.multiple_of(out_tile * t + b * bs, bs), bs)
                if on_diag and a < b:
                    hi_ref[pair, rows, cols] = jnp.zeros((bs, bs), BF16)
                    lo_ref[pair, rows, cols] = jnp.zeros((bs, bs), BF16)
                    continue
                block = held[slot, a, pl.ds(tile_col * sh.per + b, bs, stride=blocks), :]
                if on_diag and a == b:
                    block = block * on_diagonal
                high, low = split(block)
                hi_ref[pair, rows, cols] = high
                lo_ref[pair, rows, cols] = low

    for number in range(min(slots, len(strips))):
        fetch(number).start()
    for number, (pair, tile_row, first, count) in enumerate(strips):
        slot = number % slots
        fetch(number).wait()

        def step(j, carry):
            tile(slot, pair, j, first + j, False)
            return carry

        lax.fori_loop(0, tile_row, step, 0)
        tile(slot, pair, tile_row, first + tile_row, True)
        if number + slots < len(strips):
            fetch(number + slots).start()
        strip_product(sh, hi_ref, lo_ref, halves, total, pair, tile_row, first, count)
    for m, out in enumerate(out_refs):
        out[...] = total[unit_rows(sh, index_ref[3] ^ m), :]


def strip_product(sh, hi_ref, lo_ref, halves, total, pair, tile_row, first, count):
    k, t = sh.k, sh.tile
    cols = slice(first * t, (first + count) * t)
    both = dot(hi_ref[pair, :, cols], halves[: count * t, :])
    both += dot(lo_ref[pair, :, cols], halves[: count * t, :])
    total[tile_row * t : (tile_row + 1) * t, :] = both[:, :k] + both[:, k:]


def resident(value):
    return pltpu.with_memory_space_constraint(value, pltpu.VMEM)


def pack(sh, index, stored, halves, after, group):
    view = stored.reshape(sh.col_blocks, sh.groups, sh.bs * sh.col_blocks, sh.bs)
    shape = (sh.pairs, sh.tile, sh.width)
    size = sh.pairs * sh.tile * sh.width
    piece = jax.ShapeDtypeStruct((sh.unit, sh.k), F32)
    got = pl.pallas_call(
        functools.partial(pack_kernel, sh, group),
        in_specs=[SCALARS, ANYWHERE, WHOLE, ANYWHERE],
        out_specs=[WHOLE] * (2 + sh.rows_n),
        out_shape=[pltpu.VMEM(shape, BF16), pltpu.VMEM(shape, BF16), *[piece] * sh.rows_n],
        scratch_shapes=[
            pltpu.VMEM((3, sh.per, sh.bs * sh.col_blocks, sh.bs), F32),
            pltpu.VMEM((sh.colset, sh.k), F32),
            pltpu.SemaphoreType.DMA((3,)),
        ],
        compiler_params=params(13),
        cost_estimate=pl.CostEstimate(flops=40 * size, bytes_accessed=8 * size, transcendentals=0),
        name="pack_lower",
    )(index, view, resident(halves), after)
    return got[:2], got[2:]


def combined(first, second, weights):
    k = first.shape[-1]
    high, low = split(jnp.concatenate([first, second], axis=1))
    both = dot(high, weights[...]) + dot(low, weights[...])
    return both[:, :k] + both[:, k:]


def unit_rows(sh, position):
    return pl.ds(pl.multiple_of(position * sh.unit, 8), sh.unit)


def halves_kernel(sh, mixing, *refs):
    refs = list(refs)
    index_ref, start_ref = refs.pop(0), refs.pop(0)
    if mixing:
        image_refs, weight_ref = refs[: sh.rows_n], refs[sh.rows_n]
        halves, vector_ref = refs[sh.rows_n + 1 :]
        for m, image in enumerate(image_refs):
            where = unit_rows(sh, index_ref[0] ^ m)
            vector_ref[where, :] = combined(start_ref[where, :], image[...], weight_ref)
        source = vector_ref
    else:
        (halves,) = refs
        source = start_ref
    high, low = split(source[...])
    halves[:, : sh.k] = high
    halves[:, sh.k :] = low


def column_halves(sh, index, start, images=None, weights=None):
    mixing = images is not None
    outs = [pltpu.VMEM((sh.colset, 2 * sh.k), BF16)]
    extra = []
    if mixing:
        outs.append(jax.ShapeDtypeStruct((sh.colset, sh.k), F32))
        extra = [*images, weights]
    got = pl.pallas_call(
        functools.partial(halves_kernel, sh, mixing),
        in_specs=[SCALARS, WHOLE, *[WHOLE] * len(extra)],
        out_specs=[WHOLE] * len(outs),
        out_shape=outs,
        compiler_params=params(),
        name="column_halves",
    )(index, start, *extra)
    return got if mixing else (got[0], start)


def rows_kernel(sh, index_ref, hi_ref, lo_ref, halves, after_ref, *refs):
    out_refs, total = refs[:-1], refs[-1]
    for pair in range(sh.pairs):
        for strip in sh.strips(pair):
            strip_product(sh, hi_ref, lo_ref, halves, total, pair, *strip)
    for m, out in enumerate(out_refs):
        out[...] = total[unit_rows(sh, index_ref[3] ^ m), :]


def product_cost(sh):
    size = sh.pairs * sh.tile * sh.width
    return pl.CostEstimate(flops=40 * size * sh.k, bytes_accessed=4 * size, transcendentals=0)


def apply_rows(sh, index, packed, halves, after):
    piece = jax.ShapeDtypeStruct((sh.unit, sh.k), F32)
    return pl.pallas_call(
        functools.partial(rows_kernel, sh),
        in_specs=[SCALARS, WHOLE, WHOLE, WHOLE, ANYWHERE],
        out_specs=[WHOLE] * sh.rows_n,
        out_shape=[piece] * sh.rows_n,
        scratch_shapes=[pltpu.VMEM((sh.colset, sh.k), F32)],
        compiler_params=params(),
        cost_estimate=product_cost(sh),
        name="lower_times",
    )(index, *map(resident, packed), resident(halves), after)


def cols_kernel(sh, mixing, first_call, last_call, *refs):
    refs = list(refs)
    index_ref, hi_ref, lo_ref = refs[:3]
    del refs[:3]
    start_refs = [refs.pop(0) for _ in range(sh.rows_n)]
    image_refs = [refs.pop(0) for _ in range(sh.rows_n)] if mixing else []
    weight_ref = refs.pop(0) if mixing else None
    before_ref = None if first_call else refs.pop(0)
    column_ref = refs.pop(0) if last_call else None
    refs.pop(0)
    if last_call:
        out_refs = [refs.pop(0) for _ in range(sh.rows_n)]
        curve_ref = refs.pop(0)
        vector, total, turned = refs
    else:
        total, vector = refs
    k, t = sh.k, sh.tile
    for m in range(sh.rows_n):
        where = unit_rows(sh, index_ref[3] ^ m)
        if mixing:
            vector[where, :] = combined(start_refs[m][...], image_refs[m][...], weight_ref)
        else:
            vector[where, :] = start_refs[m][...]
    total[...] = jnp.zeros_like(total) if first_call else before_ref[...]
    for pair in range(sh.pairs):
        for tile_row, first, count in sh.strips(pair):
            high, low = split(vector[tile_row * t : (tile_row + 1) * t, :].T)
            stacked = jnp.concatenate([high, low], axis=0)
            for j in range(count):
                cols = slice((first + j) * t, (first + j + 1) * t)
                both = dot(stacked, hi_ref[pair, :, cols]) + dot(stacked, lo_ref[pair, :, cols])
                total[:, j * t : (j + 1) * t] += both[:k] + both[k:]
    if last_call:
        turned[...] = total[...].T
        for m, out in enumerate(out_refs):
            out[...] = turned[unit_rows(sh, index_ref[0] ^ m), :]
        curve_ref[...] = jnp.dot(
            total[...], column_ref[...], precision=HIGHEST, preferred_element_type=F32
        )


def apply_cols(sh, index, packed, starts, after, images=(), weights=None, before=None, column=None):
    mixing, last_call = bool(images), column is not None
    operands = [*starts, *images]
    if before is not None:
        before = resident(before)
    operands += [value for value in (weights, before, column) if value is not None]
    piece = jax.ShapeDtypeStruct((sh.unit, sh.k), F32)
    sums = (sh.k, sh.colset)
    vector = pltpu.VMEM((sh.colset, sh.k), F32)
    if last_call:
        outs = [piece] * sh.rows_n + [jax.ShapeDtypeStruct((sh.k, sh.k), F32)]
        scratch = [vector, pltpu.VMEM(sums, F32), vector]
    else:
        outs = [pltpu.VMEM(sums, F32)]
        scratch = [vector]
    got = pl.pallas_call(
        functools.partial(cols_kernel, sh, mixing, before is None, last_call),
        in_specs=[SCALARS, WHOLE, WHOLE, *[WHOLE] * len(operands), ANYWHERE],
        out_specs=[WHOLE] * len(outs),
        out_shape=outs,
        scratch_shapes=scratch,
        compiler_params=params(),
        cost_estimate=product_cost(sh),
        name="upper_times",
    )(index, *map(resident, packed), *operands, after)
    return (got[: sh.rows_n], got[sh.rows_n]) if last_call else got[0]


def solve_kernel(symmetric, panel, matrix_ref, target_ref, out_ref):
    size = matrix_ref.shape[0]
    matrix, target = matrix_ref[...], target_ref[...]
    if not symmetric:
        matrix = matrix + matrix.T
    rows = lax.broadcasted_iota(jnp.int32, (size, size), 0)
    for first in range(0, size, panel):
        spread = [
            jnp.broadcast_to(matrix[:, first + i : first + i + 1], (size, size))
            for i in range(panel)
        ]
        for i in range(panel):
            pivot = slice(first + i, first + i + 1)
            here, column = rows == first + i, spread[i]
            inverse = 1.0 / column[pivot, :]

            def eliminate(value):
                scaled = value[pivot, :] * inverse
                return jnp.where(here, scaled, value - column * scaled)

            for later in range(i + 1, panel):
                spread[later] = eliminate(spread[later])
            matrix, target = eliminate(matrix), eliminate(target)
    out_ref[...] = target


def solve(matrix, target, symmetric):
    return pl.pallas_call(
        functools.partial(solve_kernel, symmetric, 8),
        in_specs=[WHOLE, WHOLE],
        out_specs=WHOLE,
        out_shape=jax.ShapeDtypeStruct(target.shape, F32),
        compiler_params=params(),
        cost_estimate=pl.CostEstimate(
            flops=1 << 32, bytes_accessed=1 << 17, transcendentals=0
        ),
        name="solve_spd",
    )(matrix, target)


def weights_kernel(inverse_ref, gram_ref, step_ref, out_ref):
    k = step_ref.shape[-1]
    mixed = jnp.dot(
        inverse_ref[...], gram_ref[...], precision=HIGHEST, preferred_element_type=F32
    )
    rows = lax.broadcasted_iota(jnp.int32, (k, k), 0)
    cols = lax.broadcasted_iota(jnp.int32, (k, k), 1)
    mixed = jnp.where(rows == cols, mixed + 1.0, mixed)
    for base, value in ((0, mixed), (k, -step_ref[...])):
        high, low = split(value)
        out_ref[base : base + k, :k] = high
        out_ref[base : base + k, k:] = low


def next_weights(inverse, gram_next, step_size):
    k = step_size.shape[-1]
    return pl.pallas_call(
        weights_kernel,
        in_specs=[WHOLE] * 3,
        out_specs=WHOLE,
        out_shape=jax.ShapeDtypeStruct((2 * k, 2 * k), BF16),
        compiler_params=params(),
        name="next_weights",
    )(inverse, gram_next, step_size)


def order_kernel(sh, index_ref, *refs):
    out_ref = refs[-1]
    for m, piece in enumerate(refs[:-1]):
        out_ref[unit_rows(sh, index_ref[0] ^ m), :] = piece[...]


def in_order(sh, index, pieces):
    return pl.pallas_call(
        functools.partial(order_kernel, sh),
        in_specs=[SCALARS, *[WHOLE] * len(pieces)],
        out_specs=WHOLE,
        out_shape=jax.ShapeDtypeStruct((sh.colset, sh.k), F32),
        compiler_params=params(),
        name="in_order",
    )(index, *pieces)


def all_cols(sh, index, packed, column, starts, after, images=None, weights=None):
    before = None
    for group in range(sh.groups):
        near = slice(group * sh.rows_n, (group + 1) * sh.rows_n)
        before = apply_cols(
            sh,
            index,
            packed[group],
            starts[near],
            after,
            images=images[near] if images else (),
            weights=weights,
            before=before,
            column=column if group == sh.groups - 1 else None,
        )
    return before


def steps(stored, rhs):
    row_index = lax.axis_index("row")
    col_index = lax.axis_index("col")
    rows_n = lax.axis_size("row")
    cols_n = lax.axis_size("col")
    sh = Shape(stored, rhs, rows_n, cols_n)
    groups = range(sh.groups)
    own_group = col_index // rows_n
    index = jnp.stack([row_index, col_index, own_group, col_index % rows_n]).astype(jnp.int32)

    start = rhs.reshape(sh.colset, sh.k)
    start_piece = lax.dynamic_slice_in_dim(start, row_index * sh.unit, sh.unit, 0)
    start_rows = gather_col(swap(start_piece))
    halves, _ = column_halves(sh, index, start)
    packed, parts = [None] * sh.groups, [None] * sh.groups
    after = start
    for group in reversed(groups):
        packed[group], parts[group] = pack(sh, index, stored, halves, after, group)
        after = parts[group][0]
    row_parts = [part for share in parts for part in share]
    col_parts, curve = all_cols(sh, index, packed, start, start_rows, after)
    row_piece = scatter_col(row_parts)
    both = jnp.concatenate([curve, gram(start_piece, start_piece)], axis=0)
    both = sum_over(both, "all")
    curve, gram_now = both[: sh.k], both[sh.k :]
    step_size = solve(curve, gram_now, False)
    inverse = solve(gram_now, jnp.eye(sh.k, dtype=F32), True)
    col_piece = scatter_row(col_parts)
    image_far = row_piece + swap(col_piece)
    image_piece = col_piece + swap(row_piece)
    image_rows = gather_col(image_far)
    image_cols = gather_row(image_piece)
    residual_piece = start_piece - mix(image_piece, step_size)
    gram_next = sum_over(gram(residual_piece, residual_piece), "all")

    weights = next_weights(inverse, gram_next, step_size)
    halves, direction = column_halves(sh, index, start, image_cols, weights)
    after = halves
    for group in reversed(groups):
        parts[group] = apply_rows(sh, index, packed[group], halves, after)
        after = parts[group][0]
    row_parts = [part for share in parts for part in share]
    col_parts, curve = all_cols(
        sh, index, packed, direction, start_rows, after, image_rows, weights
    )
    row_piece = scatter_col(row_parts)
    curve = sum_over(curve, "all")
    last_step = solve(curve, gram_next, False)
    answer = mix(start, step_size)
    residual = start - mix(in_order(sh, index, image_cols), step_size)
    image_piece = scatter_row(col_parts) + swap(row_piece)
    last_image = in_order(sh, index, gather_row(image_piece))
    answer = answer + mix(direction, last_step)
    residual = residual - mix(last_image, last_step)
    return answer.reshape(rhs.shape), residual.reshape(rhs.shape)


def solution(mesh):
    placed = (P(None, "row", None, None, "col", None), P(None, "col", None, None))
    return jax.shard_map(
        steps,
        mesh=mesh,
        in_specs=placed,
        out_specs=(P(None, "col", None, None), P(None, "col", None, None)),
        check_vma=False,
    )
```

```python
import functools

import jax
import jax.numpy as jnp
from jax import lax
from jax.experimental import pallas as pl
from jax.experimental.pallas import tpu as pltpu
from jax.sharding import PartitionSpec as P


HIGHEST = lax.Precision.HIGHEST
F32 = jnp.float32
BF16 = jnp.bfloat16
WHOLE = pl.BlockSpec(memory_space=pltpu.VMEM)
SCALARS = pl.BlockSpec(memory_space=pltpu.SMEM)
ANYWHERE = pl.BlockSpec(memory_space=pl.ANY)


def params(mebibytes=8):
    return pltpu.CompilerParams(vmem_limit_bytes=mebibytes << 20)


def exchange(value, axis, mask):
    pairs = [(source, source ^ mask) for source in range(lax.axis_size(axis))]
    return lax.ppermute(value, axis, pairs)


def swap(value):
    rows_n = lax.axis_size("row")
    cols_n = lax.axis_size("col")
    pairs = []
    for r in range(rows_n):
        for c in range(cols_n):
            h, q = divmod(c, rows_n)
            pairs.append((r * cols_n + c, q * cols_n + h * rows_n + r))
    return lax.ppermute(value, ("row", "col"), pairs)


def gather_col(piece):
    cols_n = lax.axis_size("col")
    got = {0: piece}
    for m in sorted(range(2, cols_n, 2), reverse=True):
        got[m] = exchange(piece, "col", m)
    got[1] = exchange(piece, "col", 1)
    for m in range(2, cols_n, 2):
        got[m + 1] = exchange(got[m], "col", 1)
    return [got[m] for m in range(cols_n)]


def scatter_col(pieces):
    cols_n = len(pieces)
    order = sorted(range(0, cols_n, 2), reverse=True)
    arrived = {m: exchange(pieces[m + 1], "col", 1) for m in order}
    total = None
    for m in order:
        part = pieces[m] + arrived[m]
        if m:
            part = exchange(part, "col", m)
        total = part if total is None else total + part
    return total


def gather_row(piece):
    rows_n = lax.axis_size("row")
    got = {0: piece}
    mask = rows_n // 2
    while mask:
        for m in list(got):
            got[m + mask] = exchange(got[m], "row", mask)
        mask //= 2
    return [got[m] for m in range(rows_n)]


def scatter_row(pieces):
    rows_n = len(pieces)
    held = dict(enumerate(pieces))
    mask = 1
    while mask < rows_n:
        sent = {m: exchange(held[m], "row", mask) for m in held if m & mask}
        held = {m: held[m] + sent[m | mask] for m in held if not m & mask}
        mask *= 2
    return held[0]


def sum_over(value):
    cols_n = lax.axis_size("col")
    col_bits = [("col", 1 << b) for b in range(cols_n.bit_length() - 1)]
    row_bits = [("row", 1 << b) for b in range(lax.axis_size("row").bit_length() - 1)]
    rest = [col_bits[0], *row_bits[1:], *col_bits[1:]]
    stages = [row_bits[:1], *[rest[b : b + 2] for b in range(0, len(rest), 2)]]
    devices = cols_n * lax.axis_size("row")

    def send(bits):
        mask = sum(size * (cols_n if axis == "row" else 1) for axis, size in bits)
        pairs = [(source, source ^ mask) for source in range(devices)]
        return lax.ppermute(value, ("row", "col"), pairs)

    for bits in stages:
        if len(bits) == 1:
            value = value + send(bits)
        else:
            near, far = send(bits[:1]), send(bits[1:])
            value = (value + near) + (far + send(bits))
    return value


def gram(left_side, right_side):
    return jnp.einsum(
        "nk,nl->kl", left_side, right_side, precision=HIGHEST, preferred_element_type=F32
    )


def mix(vectors, matrix):
    return jnp.dot(vectors, matrix, precision=HIGHEST, preferred_element_type=F32)


def split(value):
    high = value.astype(BF16)
    return high, (value - high.astype(F32)).astype(BF16)


def dot(left_side, right_side):
    return jnp.dot(left_side, right_side, preferred_element_type=F32)


class Shape:
    def __init__(self, stored, rhs, rows_n, cols_n):
        self.rows_n, self.cols_n = rows_n, cols_n
        self.groups = cols_n // rows_n
        self.bs = stored.shape[2]
        self.col_blocks = stored.shape[3]
        self.k = rhs.shape[-1]
        self.per = 2 if self.col_blocks % 2 == 0 else 1
        self.tile = self.per * self.bs
        self.n = self.col_blocks // self.per
        self.odd = self.n % 2
        self.pairs = (self.n + self.odd) // 2
        self.width = (self.n + 1 - self.odd) * self.tile
        self.colset = self.col_blocks * self.bs
        self.unit = self.colset // rows_n

    def strips(self, pair):
        out = [(self.n - 1 - pair, 0, self.n - pair)]
        if pair - self.odd >= 0:
            out.append((pair - self.odd, self.n - pair, pair - self.odd + 1))
        return out


def pack_kernel(sh, group, index_ref, stored_ref, halves, after_ref, *refs):
    hi_ref, lo_ref = refs[0], refs[1]
    out_refs, (held, total, sems) = refs[2:-3], refs[-3:]
    blocks, bs, t = sh.col_blocks, sh.bs, sh.tile
    strips = [(pair, *strip) for pair in range(sh.pairs) for strip in sh.strips(pair)]
    slots = held.shape[0]
    offset = (index_ref[2] ^ group) * sh.rows_n + index_ref[0] - index_ref[1]
    on_diagonal = jnp.where(offset > 0, 1.0, jnp.where(offset == 0, 0.5, 0.0)).astype(F32)

    def fetch(number):
        tile_row = strips[number][1]
        slot = number % slots
        source = stored_ref.at[pl.ds(tile_row * sh.per, sh.per), index_ref[2] ^ group]
        return pltpu.make_async_copy(source, held.at[slot], sems.at[slot])

    def tile(slot, pair, tile_col, out_tile, on_diag):
        for a in range(sh.per):
            for b in range(sh.per):
                rows = slice(a * bs, (a + 1) * bs)
                cols = pl.ds(pl.multiple_of(out_tile * t + b * bs, bs), bs)
                if on_diag and a < b:
                    hi_ref[pair, rows, cols] = jnp.zeros((bs, bs), BF16)
                    lo_ref[pair, rows, cols] = jnp.zeros((bs, bs), BF16)
                    continue
                block = held[slot, a, pl.ds(tile_col * sh.per + b, bs, stride=blocks), :]
                if on_diag and a == b:
                    block = block * on_diagonal
                high, low = split(block)
                hi_ref[pair, rows, cols] = high
                lo_ref[pair, rows, cols] = low

    for number in range(min(slots, len(strips))):
        fetch(number).start()
    for number, (pair, tile_row, first, count) in enumerate(strips):
        slot = number % slots
        fetch(number).wait()

        def step(j, carry):
            tile(slot, pair, j, first + j, False)
            return carry

        lax.fori_loop(0, tile_row, step, 0)
        tile(slot, pair, tile_row, first + tile_row, True)
        if number + slots < len(strips):
            fetch(number + slots).start()
        strip_product(sh, hi_ref, lo_ref, halves, total, pair, tile_row, first, count)
    for m, out in enumerate(out_refs):
        out[...] = total[unit_rows(sh, index_ref[3] ^ m), :]


def strip_product(sh, hi_ref, lo_ref, halves, total, pair, tile_row, first, count):
    k, t = sh.k, sh.tile
    cols = slice(first * t, (first + count) * t)
    both = dot(hi_ref[pair, :, cols], halves[: count * t, :])
    both += dot(lo_ref[pair, :, cols], halves[: count * t, :])
    total[tile_row * t : (tile_row + 1) * t, :] = both[:, :k] + both[:, k:]


def resident(value):
    return pltpu.with_memory_space_constraint(value, pltpu.VMEM)


def pack(sh, index, stored, halves, after, group):
    view = stored.reshape(sh.col_blocks, sh.groups, sh.bs * sh.col_blocks, sh.bs)
    shape = (sh.pairs, sh.tile, sh.width)
    size = sh.pairs * sh.tile * sh.width
    piece = jax.ShapeDtypeStruct((sh.unit, sh.k), F32)
    got = pl.pallas_call(
        functools.partial(pack_kernel, sh, group),
        in_specs=[SCALARS, ANYWHERE, WHOLE, ANYWHERE],
        out_specs=[WHOLE] * (2 + sh.rows_n),
        out_shape=[pltpu.VMEM(shape, BF16), pltpu.VMEM(shape, BF16), *[piece] * sh.rows_n],
        scratch_shapes=[
            pltpu.VMEM((3, sh.per, sh.bs * sh.col_blocks, sh.bs), F32),
            pltpu.VMEM((sh.colset, sh.k), F32),
            pltpu.SemaphoreType.DMA((3,)),
        ],
        compiler_params=params(13),
        cost_estimate=pl.CostEstimate(flops=40 * size, bytes_accessed=8 * size, transcendentals=0),
        name="pack_lower",
    )(index, view, resident(halves), after)
    return got[:2], got[2:]


def combined(first, second, weights):
    k = first.shape[-1]
    high, low = split(jnp.concatenate([first, second], axis=1))
    both = dot(high, weights[...]) + dot(low, weights[...])
    return both[:, :k] + both[:, k:]


def unit_rows(sh, position):
    return pl.ds(pl.multiple_of(position * sh.unit, 8), sh.unit)


def halves_kernel(sh, mixing, *refs):
    refs = list(refs)
    index_ref, start_ref = refs.pop(0), refs.pop(0)
    if mixing:
        image_refs, weight_ref = refs[: sh.rows_n], refs[sh.rows_n]
        halves, vector_ref = refs[sh.rows_n + 1 :]
        for m, image in enumerate(image_refs):
            where = unit_rows(sh, index_ref[0] ^ m)
            vector_ref[where, :] = combined(start_ref[where, :], image[...], weight_ref)
        source = vector_ref
    else:
        (halves,) = refs
        source = start_ref
    high, low = split(source[...])
    halves[:, : sh.k] = high
    halves[:, sh.k :] = low


def column_halves(sh, index, start, images=None, weights=None):
    mixing = images is not None
    outs = [pltpu.VMEM((sh.colset, 2 * sh.k), BF16)]
    extra = []
    if mixing:
        outs.append(jax.ShapeDtypeStruct((sh.colset, sh.k), F32))
        extra = [*images, weights]
    got = pl.pallas_call(
        functools.partial(halves_kernel, sh, mixing),
        in_specs=[SCALARS, WHOLE, *[WHOLE] * len(extra)],
        out_specs=[WHOLE] * len(outs),
        out_shape=outs,
        compiler_params=params(),
        name="column_halves",
    )(index, start, *extra)
    return got if mixing else (got[0], start)


def rows_kernel(sh, index_ref, hi_ref, lo_ref, halves, after_ref, *refs):
    out_refs, total = refs[:-1], refs[-1]
    for pair in range(sh.pairs):
        for strip in sh.strips(pair):
            strip_product(sh, hi_ref, lo_ref, halves, total, pair, *strip)
    for m, out in enumerate(out_refs):
        out[...] = total[unit_rows(sh, index_ref[3] ^ m), :]


def product_cost(sh):
    size = sh.pairs * sh.tile * sh.width
    return pl.CostEstimate(flops=40 * size * sh.k, bytes_accessed=4 * size, transcendentals=0)


def apply_rows(sh, index, packed, halves, after):
    piece = jax.ShapeDtypeStruct((sh.unit, sh.k), F32)
    return pl.pallas_call(
        functools.partial(rows_kernel, sh),
        in_specs=[SCALARS, WHOLE, WHOLE, WHOLE, ANYWHERE],
        out_specs=[WHOLE] * sh.rows_n,
        out_shape=[piece] * sh.rows_n,
        scratch_shapes=[pltpu.VMEM((sh.colset, sh.k), F32)],
        compiler_params=params(),
        cost_estimate=product_cost(sh),
        name="lower_times",
    )(index, *map(resident, packed), resident(halves), after)


def cols_kernel(sh, mixing, first_call, last_call, *refs):
    refs = list(refs)
    index_ref, hi_ref, lo_ref = refs[:3]
    del refs[:3]
    start_refs = [refs.pop(0) for _ in range(sh.rows_n)]
    image_refs = [refs.pop(0) for _ in range(sh.rows_n)] if mixing else []
    weight_ref = refs.pop(0) if mixing else None
    before_ref = None if first_call else refs.pop(0)
    column_ref = refs.pop(0) if last_call else None
    refs.pop(0)
    if last_call:
        out_refs = [refs.pop(0) for _ in range(sh.rows_n)]
        curve_ref = refs.pop(0)
        vector, total, turned = refs
    else:
        total, vector = refs
    k, t = sh.k, sh.tile
    for m in range(sh.rows_n):
        where = unit_rows(sh, index_ref[3] ^ m)
        if mixing:
            vector[where, :] = combined(start_refs[m][...], image_refs[m][...], weight_ref)
        else:
            vector[where, :] = start_refs[m][...]
    total[...] = jnp.zeros_like(total) if first_call else before_ref[...]
    for pair in range(sh.pairs):
        for tile_row, first, count in sh.strips(pair):
            high, low = split(vector[tile_row * t : (tile_row + 1) * t, :].T)
            stacked = jnp.concatenate([high, low], axis=0)
            for j in range(count):
                cols = slice((first + j) * t, (first + j + 1) * t)
                both = dot(stacked, hi_ref[pair, :, cols]) + dot(stacked, lo_ref[pair, :, cols])
                total[:, j * t : (j + 1) * t] += both[:k] + both[k:]
    if last_call:
        turned[...] = total[...].T
        for m, out in enumerate(out_refs):
            out[...] = turned[unit_rows(sh, index_ref[0] ^ m), :]
        curve_ref[...] = jnp.dot(
            total[...], column_ref[...], precision=HIGHEST, preferred_element_type=F32
        )


def apply_cols(sh, index, packed, starts, after, images=(), weights=None, before=None, column=None):
    mixing, last_call = bool(images), column is not None
    operands = [*starts, *images]
    if before is not None:
        before = resident(before)
    operands += [value for value in (weights, before, column) if value is not None]
    piece = jax.ShapeDtypeStruct((sh.unit, sh.k), F32)
    sums = (sh.k, sh.colset)
    vector = pltpu.VMEM((sh.colset, sh.k), F32)
    if last_call:
        outs = [piece] * sh.rows_n + [jax.ShapeDtypeStruct((sh.k, sh.k), F32)]
        scratch = [vector, pltpu.VMEM(sums, F32), vector]
    else:
        outs = [pltpu.VMEM(sums, F32)]
        scratch = [vector]
    got = pl.pallas_call(
        functools.partial(cols_kernel, sh, mixing, before is None, last_call),
        in_specs=[SCALARS, WHOLE, WHOLE, *[WHOLE] * len(operands), ANYWHERE],
        out_specs=[WHOLE] * len(outs),
        out_shape=outs,
        scratch_shapes=scratch,
        compiler_params=params(),
        cost_estimate=product_cost(sh),
        name="upper_times",
    )(index, *map(resident, packed), *operands, after)
    return (got[: sh.rows_n], got[sh.rows_n]) if last_call else got[0]


def solve_kernel(symmetric, panel, matrix_ref, target_ref, out_ref):
    size = matrix_ref.shape[0]
    matrix, target = matrix_ref[...], target_ref[...]
    if not symmetric:
        matrix = matrix + matrix.T
    rows = lax.broadcasted_iota(jnp.int32, (size, size), 0)
    for first in range(0, size, panel):
        spread = [
            jnp.broadcast_to(matrix[:, first + i : first + i + 1], (size, size))
            for i in range(panel)
        ]
        for i in range(panel):
            pivot = slice(first + i, first + i + 1)
            here, column = rows == first + i, spread[i]
            inverse = 1.0 / column[pivot, :]

            def eliminate(value):
                scaled = value[pivot, :] * inverse
                return jnp.where(here, scaled, value - column * scaled)

            for later in range(i + 1, panel):
                spread[later] = eliminate(spread[later])
            matrix, target = eliminate(matrix), eliminate(target)
    out_ref[...] = target


def solve(matrix, target, symmetric):
    return pl.pallas_call(
        functools.partial(solve_kernel, symmetric, 8),
        in_specs=[WHOLE, WHOLE],
        out_specs=WHOLE,
        out_shape=jax.ShapeDtypeStruct(target.shape, F32),
        compiler_params=params(),
        cost_estimate=pl.CostEstimate(
            flops=1 << 32, bytes_accessed=1 << 17, transcendentals=0
        ),
        name="solve_spd",
    )(matrix, target)


def weights_kernel(inverse_ref, gram_ref, step_ref, out_ref):
    k = step_ref.shape[-1]
    mixed = jnp.dot(
        inverse_ref[...], gram_ref[...], precision=HIGHEST, preferred_element_type=F32
    )
    rows = lax.broadcasted_iota(jnp.int32, (k, k), 0)
    cols = lax.broadcasted_iota(jnp.int32, (k, k), 1)
    mixed = jnp.where(rows == cols, mixed + 1.0, mixed)
    for base, value in ((0, mixed), (k, -step_ref[...])):
        high, low = split(value)
        out_ref[base : base + k, :k] = high
        out_ref[base : base + k, k:] = low


def next_weights(inverse, gram_next, step_size):
    k = step_size.shape[-1]
    return pl.pallas_call(
        weights_kernel,
        in_specs=[WHOLE] * 3,
        out_specs=WHOLE,
        out_shape=jax.ShapeDtypeStruct((2 * k, 2 * k), BF16),
        compiler_params=params(),
        name="next_weights",
    )(inverse, gram_next, step_size)


def split_three(value):
    high = value.astype(BF16)
    rest = value - high.astype(F32)
    middle = rest.astype(BF16)
    return high, middle, (rest - middle.astype(F32)).astype(BF16)


def times(vectors, matrix):
    k = matrix.shape[-1]
    high, middle, low = split_three(vectors)
    top, centre, bottom = split_three(matrix)
    pair = jnp.concatenate([top, centre], axis=1)
    both = dot(high, pair) + dot(middle, pair)
    return both[:, :k] + (both[:, k:] + (dot(high, bottom) + dot(low, top)))


def update_kernel(sh, first, index_ref, *refs):
    if first:
        start_ref, step_ref = refs[0], refs[1]
        images, (answer_ref, residual_ref) = refs[2:-2], refs[-2:]
    else:
        solved_ref, left_ref, direction_ref, step_ref = refs[:4]
        images, (answer_ref, residual_ref) = refs[4:-2], refs[-2:]
    step = step_ref[...]
    for m, image in enumerate(images):
        where = unit_rows(sh, index_ref[0] ^ m)
        if first:
            answer_ref[where, :] = times(start_ref[where, :], step)
            residual_ref[where, :] = start_ref[where, :] - times(image[...], step)
        else:
            answer_ref[where, :] = solved_ref[where, :] + times(direction_ref[where, :], step)
            residual_ref[where, :] = left_ref[where, :] - times(image[...], step)


def update(sh, index, vectors, images):
    first = len(vectors) == 2
    shape = (sh.colset, sh.k)
    outs = [pltpu.VMEM(shape, F32) if first else jax.ShapeDtypeStruct(shape, F32)] * 2
    return pl.pallas_call(
        functools.partial(update_kernel, sh, first),
        in_specs=[SCALARS, *[WHOLE] * (len(vectors) + len(images))],
        out_specs=[WHOLE] * 2,
        out_shape=outs,
        compiler_params=params(12),
        name="update",
    )(index, *vectors, *images)


def all_cols(sh, index, packed, column, starts, after, images=None, weights=None):
    before = None
    for group in range(sh.groups):
        near = slice(group * sh.rows_n, (group + 1) * sh.rows_n)
        before = apply_cols(
            sh,
            index,
            packed[group],
            starts[near],
            after,
            images=images[near] if images else (),
            weights=weights,
            before=before,
            column=column if group == sh.groups - 1 else None,
        )
    return before


def steps(stored, rhs):
    row_index = lax.axis_index("row")
    col_index = lax.axis_index("col")
    rows_n = lax.axis_size("row")
    cols_n = lax.axis_size("col")
    sh = Shape(stored, rhs, rows_n, cols_n)
    groups = range(sh.groups)
    own_group = col_index // rows_n
    index = jnp.stack([row_index, col_index, own_group, col_index % rows_n]).astype(jnp.int32)

    start = rhs.reshape(sh.colset, sh.k)
    start_piece = lax.dynamic_slice_in_dim(start, row_index * sh.unit, sh.unit, 0)
    start_rows = gather_col(swap(start_piece))
    halves, _ = column_halves(sh, index, start)
    packed, parts = [None] * sh.groups, [None] * sh.groups
    after = start
    for group in reversed(groups):
        packed[group], parts[group] = pack(sh, index, stored, halves, after, group)
        after = parts[group][0]
    row_parts = [part for share in parts for part in share]
    col_parts, curve = all_cols(sh, index, packed, start, start_rows, after)
    row_piece = scatter_col(row_parts)
    both = jnp.concatenate([curve, gram(start_piece, start_piece)], axis=0)
    both = sum_over(both)
    curve, gram_now = both[: sh.k], both[sh.k :]
    step_size = solve(curve, gram_now, False)
    inverse = solve(gram_now, jnp.eye(sh.k, dtype=F32), True)
    col_piece = scatter_row(col_parts)
    image_far = row_piece + swap(col_piece)
    image_piece = col_piece + swap(row_piece)
    image_rows = gather_col(image_far)
    image_cols = gather_row(image_piece)
    residual_piece = start_piece - mix(image_piece, step_size)
    gram_next = sum_over(gram(residual_piece, residual_piece))

    weights = next_weights(inverse, gram_next, step_size)
    halves, direction = column_halves(sh, index, start, image_cols, weights)
    after = halves
    for group in reversed(groups):
        parts[group] = apply_rows(sh, index, packed[group], halves, after)
        after = parts[group][0]
    row_parts = [part for share in parts for part in share]
    col_parts, curve = all_cols(
        sh, index, packed, direction, start_rows, after, image_rows, weights
    )
    row_piece = scatter_col(row_parts)
    curve = sum_over(curve)
    last_step = solve(curve, gram_next, False)
    solved, left = update(sh, index, [start, step_size], image_cols)
    image_piece = scatter_row(col_parts) + swap(row_piece)
    last_images = gather_row(image_piece)
    answer, residual = update(
        sh, index, [resident(solved), resident(left), direction, last_step], last_images
    )
    return answer.reshape(rhs.shape), residual.reshape(rhs.shape)


def solution(mesh):
    placed = (P(None, "row", None, None, "col", None), P(None, "col", None, None))
    return jax.shard_map(
        steps,
        mesh=mesh,
        in_specs=placed,
        out_specs=(P(None, "col", None, None), P(None, "col", None, None)),
        check_vma=False,
    )
```
